32 devices in a mesh: groups: 2 (over y), ctx: 4 (over z), tensor: 2 (over x), dp: 2 (over core).
Axes of the slice: x: 2, y: 2, z: 4, core: 2. Of those that a mesh axis runs over, the one named last changes fastest.
Arguments:
- tokens: bfloat16 [4, 1024, 1024], P(('groups', 'dp'), 'ctx', 'tensor'), parts along dimension 0
- w_qkv: bfloat16 [1024, 3, 1024], P(None, None, 'tensor')
- w_out: bfloat16 [1024, 1024], P('tensor'), may hold values from -0.1875 to 0.1875
- labels: int32 [4, 8, 1024], P(('groups', 'dp'), 'tensor', 'ctx'), parts along dimension 0, may hold values from 0 to 255, as said below
- grad_out: bfloat16 [4, 1024, 1024], P(('groups', 'dp'), 'ctx', 'tensor'), parts along dimension 0, may hold values from -6 to 6
Outputs:
- attended: bfloat16 [4, 1024, 1024], P(('groups', 'dp'), 'ctx', 'tensor'), parts along dimension 0
- grad_tokens: bfloat16 [4, 1024, 1024], P(('groups', 'dp'), 'ctx', 'tensor'), parts along dimension 0
- grad_w_qkv: float32 [2048, 3, 1024], P('groups', None, 'tensor'), parts along dimension 0
- grad_w_out: float32 [2048, 1024], P(('groups', 'tensor')), parts along dimension 0
The draws below stay inside these ranges and needn't reach their ends.
There are 2 independent parts, one for each index of `groups`. The reference program is written for one: setup_inputs(seed, part) draws one part's arguments, and reference() takes and returns one part's arrays. A program takes and returns all parts, laid end to end along the dimension named above; an argument that names none is the same for every part. Nothing has to cross between parts.
Inputs may be any that keep to these rules, and one draw needn't show every extreme that they name: `labels`: cluster c of any head belongs to owner c % 4. Among the 256 tokens of one document on one index of ctx, at most 192 have, for one head, clusters of one owner; for each head one owner has exactly 192 from every such block, and the other owners share the rest of a block evenly (counts differ by at most one).
All inputs are finite; a program needn't handle non-finite values.
Results may differ from the reference program's by a relative error of at most 0.035.
The reference program's roundings to bfloat16 on the way (of `qkv`, `cotangent`, `probs`, `attention`, `dscore` and `grad_qkv`) count: a program that leaves them out, or rounds other values in their place, can miss the bound.
Values may be sent and summed in bfloat16 or wider, within the bound.
A program may use at most 64 MiB of HBM per device.

```python
import math
import jax
import jax.numpy as jnp
from jax import lax

D = 1024
H = 8
HD = 128
C = 256
TOK_DEV = 256
DOCS = 2
SEQ = 1024
CAP = 192
N_CTX = 4


def draw_labels(key, part):
    base = jax.random.fold_in(key, 23)
    hottest = jax.random.randint(jax.random.fold_in(base, 1), (H,), 0, N_CTX).astype(jnp.int32)
    rank_keys = jax.random.split(jax.random.fold_in(base, 2), DOCS * H * N_CTX)
    ranks = jax.vmap(lambda one_key: jax.random.permutation(one_key, TOK_DEV))(rank_keys)
    ranks = ranks.astype(jnp.int32).reshape(DOCS, H, N_CTX, TOK_DEV)
    hot_owner = hottest[None, :, None, None]
    spread_owner = (hot_owner + 1 + jnp.maximum(ranks - CAP, 0) % (N_CTX - 1)) % N_CTX
    owner_pick = jnp.where(ranks < CAP, hot_owner, spread_owner)
    within = jax.random.randint(jax.random.fold_in(base, 3), (DOCS, H, N_CTX, TOK_DEV), 0, C // N_CTX).astype(jnp.int32)
    chosen = owner_pick + N_CTX * within
    return chosen.reshape(DOCS, H, N_CTX * TOK_DEV).astype(jnp.int32)


def draw_tokens(key, part):
    noise_key = jax.random.fold_in(key, 31)
    noise = jax.random.normal(jax.random.fold_in(noise_key, 1), (DOCS, SEQ, D), jnp.float32)
    values = noise
    return jnp.clip(values, -30.0, 30.0).astype(jnp.bfloat16)


def draw_w_qkv(key, part):
    weight_key = jax.random.fold_in(key, 47)
    fan_scale = D ** (-0.5)
    base = jax.random.normal(jax.random.fold_in(weight_key, 1), (D, 3, H * HD), jnp.float32) * fan_scale
    values = base
    return jnp.clip(values, -6.0 * fan_scale, 6.0 * fan_scale).astype(jnp.bfloat16)


def block_scale(own_key, shape, cuts, smallest, high):
    level = 1.0
    for axis_at, blocks in cuts:
        heights = jax.random.uniform(jax.random.fold_in(jax.random.fold_in(own_key, 6), axis_at), (blocks,), jnp.float32, smallest / len(cuts), high / len(cuts))
        level = level * jnp.repeat(jnp.exp(heights), shape[axis_at] // blocks).reshape((-1,) + (1,) * (len(shape) - 1 - axis_at))
    return level


def gaussian(own_key, extent, deviation, reach, shards=(), held_as=jnp.bfloat16):
    loudness = block_scale(own_key, extent, shards, -0.22, 0.18) if shards else 1.0
    values = jax.random.normal(own_key, extent, jnp.float32) * deviation * loudness
    return jnp.minimum(jnp.maximum(values, -reach), reach).astype(held_as)


def setup_inputs(seed: int = 0, part: int = 0) -> dict:
    arg_keys = jax.random.split(jax.random.key(seed), 6)
    part_splits = jax.random.split(jax.random.fold_in(arg_keys[5], part), 6)
    tokens = draw_tokens(jax.random.fold_in(jax.random.fold_in(arg_keys[5], part), 71), part)
    w_qkv = draw_w_qkv(jax.random.fold_in(arg_keys[5], 71), part)
    w_out = gaussian(arg_keys[2], (H * HD, D), (H * HD) ** -0.5, 0.1875, ((0, 2),))
    labels = draw_labels(jax.random.fold_in(jax.random.fold_in(arg_keys[5], part), 71), part)
    grad_out = gaussian(part_splits[4], (DOCS, SEQ, D), 1.0, 6.0, ((0, 2), (1, 4), (2, 2)))
    return {"tokens": tokens, "w_qkv": w_qkv, "w_out": w_out, "labels": labels, "grad_out": grad_out}


def masked_probs(query_block, label_block, keys_in, labels_in):
    scores = jnp.dot(query_block, keys_in.T, preferred_element_type=jnp.float32) * (HD ** -0.5)
    same = label_block[:, None] == labels_in[None, :]
    scores = jnp.where(same, scores, jnp.float32(-1e30))
    top_value = jnp.max(scores, axis=1, keepdims=True)
    expo = jnp.exp(scores - top_value)
    return expo / jnp.sum(expo, axis=1, keepdims=True)


def head_pass(queries, keys_in, values_in, labels_in, cotangent):
    total = queries.shape[0]
    block_rows = math.gcd(total, 512)
    block_count = total // block_rows

    def forward_block(index):
        start = index * block_rows
        query_block = lax.dynamic_slice_in_dim(queries, start, block_rows, 0)
        label_block = lax.dynamic_slice_in_dim(labels_in, start, block_rows, 0)
        probs = masked_probs(query_block, label_block, keys_in, labels_in).astype(jnp.bfloat16)
        return jnp.dot(probs, values_in, preferred_element_type=jnp.float32).astype(jnp.bfloat16)

    attention = lax.map(forward_block, jnp.arange(block_count, dtype=jnp.int32)).reshape(total, HD)

    def backward_block(carry, index):
        grad_keys, grad_values = carry
        start = index * block_rows
        query_block = lax.dynamic_slice_in_dim(queries, start, block_rows, 0)
        label_block = lax.dynamic_slice_in_dim(labels_in, start, block_rows, 0)
        attn_block = lax.dynamic_slice_in_dim(attention, start, block_rows, 0)
        cot_block = lax.dynamic_slice_in_dim(cotangent, start, block_rows, 0)
        probs_full = masked_probs(query_block, label_block, keys_in, labels_in)
        probs = probs_full.astype(jnp.bfloat16)
        dprob = jnp.dot(cot_block, values_in.T, preferred_element_type=jnp.float32)
        delta = jnp.sum(cot_block.astype(jnp.float32) * attn_block.astype(jnp.float32), axis=1, keepdims=True)
        dscore = (probs_full * (dprob - delta) * (HD ** -0.5)).astype(jnp.bfloat16)
        grad_query = jnp.dot(dscore, keys_in, preferred_element_type=jnp.float32).astype(jnp.bfloat16)
        grad_keys = grad_keys + jnp.dot(dscore.T, query_block, preferred_element_type=jnp.float32)
        grad_values = grad_values + jnp.dot(probs.T, cot_block, preferred_element_type=jnp.float32)
        return (grad_keys, grad_values), grad_query

    empty = jnp.zeros((total, HD), jnp.float32)
    (grad_keys, grad_values), grad_queries = lax.scan(backward_block, (empty, empty), jnp.arange(block_count, dtype=jnp.int32))
    return attention, grad_queries.reshape(total, HD), grad_keys.astype(jnp.bfloat16), grad_values.astype(jnp.bfloat16)


def reference(tokens, w_qkv, w_out, labels, grad_out):
    docs, seq_len, width = tokens.shape
    heads = w_out.shape[0] // HD
    flat_rows = tokens.reshape(docs * seq_len, width)
    flat_grads = grad_out.reshape(docs * seq_len, width)
    qkv = jnp.dot(flat_rows, w_qkv.reshape(width, 3 * heads * HD), preferred_element_type=jnp.float32)
    qkv = qkv.astype(jnp.bfloat16).reshape(docs, seq_len, 3, heads, HD)
    cotangent = jnp.dot(flat_grads, w_out.T, preferred_element_type=jnp.float32).astype(jnp.bfloat16)
    cotangent = cotangent.reshape(docs, seq_len, heads, HD)

    def by_head(array):
        return jnp.transpose(array, (0, 2, 1, 3)).reshape(docs * heads, seq_len, HD)

    def per_head(inputs):
        return head_pass(inputs[0], inputs[1], inputs[2], inputs[3], inputs[4])

    stacked = (by_head(qkv[:, :, 0]), by_head(qkv[:, :, 1]), by_head(qkv[:, :, 2]),
               labels.reshape(docs * heads, seq_len), by_head(cotangent))
    attention, grad_q, grad_k, grad_v = lax.map(per_head, stacked)

    def to_rows(array):
        return jnp.transpose(array.reshape(docs, heads, seq_len, HD), (0, 2, 1, 3)).reshape(docs * seq_len, heads * HD)

    attention_rows = to_rows(attention)
    attended = jnp.dot(attention_rows, w_out, preferred_element_type=jnp.float32).astype(jnp.bfloat16)
    grad_w_out = jnp.dot(attention_rows.T, flat_grads, preferred_element_type=jnp.float32)
    grad_qkv = jnp.stack([to_rows(grad_q), to_rows(grad_k), to_rows(grad_v)], axis=1).reshape(docs * seq_len, 3 * heads * HD)
    grad_w_qkv = jnp.dot(flat_rows.T, grad_qkv, preferred_element_type=jnp.float32).reshape(width, 3, heads * HD)
    grad_tokens = jnp.dot(grad_qkv, w_qkv.reshape(width, 3 * heads * HD).T, preferred_element_type=jnp.float32)
    return (attended.reshape(docs, seq_len, width), grad_tokens.astype(jnp.bfloat16).reshape(docs, seq_len, width),
            grad_w_qkv, grad_w_out)
```

```python
import functools

import jax
import jax.numpy as jnp
from jax import lax
from jax.experimental import pallas as pl
from jax.experimental.pallas import tpu as pltpu
from jax.sharding import PartitionSpec as P

HD = 128
F32 = jnp.float32
BF16 = jnp.bfloat16


def dot_general(left, right, left_dim, right_dim):
    return lax.dot_general(
        left, right, (((left_dim,), (right_dim,)), ((), ())), preferred_element_type=F32
    )


def project_kernel(rows_ref, grads_ref, w_qkv_ref, w_out_ref, out_ref):
    heads = out_ref.shape[0]
    size = heads * HD
    for j in range(3):
        part = dot_general(rows_ref[...], w_qkv_ref[:, j * size : (j + 1) * size], 1, 0).astype(BF16)
        for h in range(heads):
            out_ref[h, :, j * HD : (j + 1) * HD] = part[:, h * HD : (h + 1) * HD]
    part = dot_general(grads_ref[...], w_out_ref[...], 1, 1).astype(BF16)
    for h in range(heads):
        out_ref[h, :, 3 * HD :] = part[:, h * HD : (h + 1) * HD]


def attention_kernel(own_keys, block_rows, x_ref, kv_ref, mark_ref, key_mark_ref, *outs):
    if own_keys:
        (y_ref, gk_acc, gv_acc) = outs
        keys = x_ref[:, HD : 2 * HD]
        values = x_ref[:, 2 * HD : 3 * HD]
    else:
        (y_ref, gkv_ref, gk_acc, gv_acc) = outs
        keys = kv_ref[:, :HD]
        values = kv_ref[:, HD:]
    key_marks = key_mark_ref[...]
    count = x_ref.shape[0] // block_rows

    def one_block(b):
        rows = pl.ds(pl.multiple_of(b * block_rows, block_rows), block_rows)
        query = x_ref[rows, :HD]
        cot = x_ref[rows, 3 * HD :]
        scores = dot_general(query, keys, 1, 1) * HD ** (-0.5)
        scores = jnp.where(mark_ref[rows, :] == key_marks, scores, F32(-1e30))
        top = jnp.max(scores, axis=1, keepdims=True)
        expo = jnp.exp(scores - top)
        full = expo * (1.0 / jnp.sum(expo, axis=1, keepdims=True))
        probs = full.astype(BF16)
        attention = dot_general(probs, values, 1, 0).astype(BF16)
        dprob = dot_general(cot, values, 1, 1)
        delta = jnp.sum(cot.astype(F32) * attention.astype(F32), axis=1, keepdims=True)
        dscore = (full * (dprob - delta) * HD ** (-0.5)).astype(BF16)
        y_ref[rows, :HD] = dot_general(dscore, keys, 1, 0).astype(BF16)
        y_ref[rows, 3 * HD :] = attention
        return dot_general(dscore, query, 0, 0), dot_general(probs, cot, 0, 0)

    if count <= 4:
        grad_keys, grad_values = one_block(0)
        for b in range(1, count):
            more_keys, more_values = one_block(b)
            grad_keys = grad_keys + more_keys
            grad_values = grad_values + more_values
    else:
        gk_acc[...] = jnp.zeros_like(gk_acc)
        gv_acc[...] = jnp.zeros_like(gv_acc)

        @pl.loop(0, count)
        def _(b):
            more_keys, more_values = one_block(b)
            gk_acc[...] += more_keys
            gv_acc[...] += more_values

        grad_keys, grad_values = gk_acc[...], gv_acc[...]
    if own_keys:
        y_ref[:, HD : 2 * HD] = grad_keys.astype(BF16)
        y_ref[:, 2 * HD : 3 * HD] = grad_values.astype(BF16)
    else:
        gkv_ref[:, :HD] = grad_keys.astype(BF16)
        gkv_ref[:, HD:] = grad_values.astype(BF16)


def finish_kernel(z_ref, rows_ref, grads_ref, w_qkv_ref, w_out_ref, out_ref, in_ref, gwq_ref, gwo_ref):
    heads = z_ref.shape[0]
    size = heads * HD
    attention = jnp.concatenate([z_ref[h, :, 3 * HD :] for h in range(heads)], axis=1)
    out_ref[...] = dot_general(attention, w_out_ref[...], 1, 0).astype(BF16)
    gwo_ref[...] = dot_general(attention, grads_ref[...], 0, 0).astype(BF16)
    total = None
    for j in range(3):
        grad = jnp.concatenate([z_ref[h, :, j * HD : (j + 1) * HD] for h in range(heads)], axis=1)
        cols = slice(j * size, (j + 1) * size)
        term = dot_general(grad, w_qkv_ref[:, cols], 1, 1)
        total = term if total is None else total + term
        gwq_ref[:, cols] = dot_general(rows_ref[...], grad, 0, 0).astype(BF16)
    in_ref[...] = total.astype(BF16)


def remote(source, target, send_sem, recv_sem, device):
    return pltpu.make_async_remote_copy(
        src_ref=source,
        dst_ref=target,
        send_sem=send_sem,
        recv_sem=recv_sem,
        device_id=device,
        device_id_type=pl.DeviceIdType.MESH,
    )


LOG2E = 1.4426950408889634
PIECES = 2


def layer_kernel(
    tok_ref, gro_ref, w3_hbm, wo_hbm, lab_ref,
    att_out, tokgrad_out, gwq_out, gwo_out,
    w3_ref, wo_ref, tok, grd, qkv, cot, marks, label_rows, label_cols, lse, att,
    near, far, grads, own_w, other_w, x_send, x_recv,
    sz, rz, sx, rx, sl, rl, sw, rw, st, rt, wsem,
):
    z = lax.axis_index("ctx")
    x = lax.axis_index("tensor")
    c = lax.axis_index("dp")
    count, half = tok_ref.shape
    scale = HD ** (-0.5)
    other_x = 1 - x
    x_dev = {"tensor": other_x}
    c_dev = {"dp": 1 - c}
    peers = [lax.rem(z + d, 4) for d in range(1, 4)]
    side = z // 2
    mate = z + 1 - 2 * (z % 2)
    inner = jnp.logical_or(z == 1, z == 2)
    cross_dev = {"ctx": 3 - z}
    mate_dev = {"ctx": mate}
    places = (z, mate, 2 - side, 3 - 3 * side)
    OWN, MATE, NEXT, LAST = range(4)

    w_copies = [
        pltpu.make_async_copy(w3_hbm, w3_ref, wsem.at[0]),
        pltpu.make_async_copy(wo_hbm, wo_ref, wsem.at[1]),
    ]
    for copy in w_copies:
        copy.start()
    barrier = pltpu.get_barrier_semaphore()
    for device in [{"ctx": p} for p in peers] + [x_dev, c_dev]:
        pl.semaphore_signal(barrier, inc=1, device_id=device, device_id_type=pl.DeviceIdType.MESH)
    pl.semaphore_wait(barrier, 5)

    def block(index, size):
        return pl.ds(pl.multiple_of(index * size, size), size)

    piece = count // PIECES
    inputs = (tok_ref, gro_ref)
    gathered = (tok, grd)
    T, G = 0, 1
    mine = block(x, half)

    def rows(p):
        return slice(p * piece, (p + 1) * piece)

    def home(array, k, p):
        return gathered[array].at[places[k], rows(p), mine]

    def z_copy(array, k, p, slot, route, device):
        source = inputs[array].at[rows(p)] if k == OWN else home(array, k, p)
        return remote(source, home(array, k, p), sz.at[array, route, p], rz.at[array, slot, p], device)

    def z_in(array, k, p):
        return remote(home(array, k, p), home(array, k, p), sz.at[array, 0, p], rz.at[array, k, p], mate_dev)

    def x_copy(array, k, p):
        source = inputs[array].at[rows(p)] if k == OWN else home(array, k, p)
        return remote(source, home(array, k, p), sx.at[array, k, p], rx.at[array, k, p], x_dev)

    def x_in(array, k, p):
        there = gathered[array].at[places[k], rows(p), block(other_x, half)]
        return remote(there, there, sx.at[array, k, p], rx.at[array, k, p], x_dev)

    def own_to_mate(array, p):
        return z_copy(array, OWN, p, MATE, 0, mate_dev)

    def own_to_cross(array, p):
        return z_copy(array, OWN, p, NEXT, 1, cross_dev)

    def relay(array, k, p):
        if k == MATE:
            return z_copy(array, MATE, p, LAST, 2, cross_dev)
        return z_copy(array, k, p, k, k + 1, mate_dev)

    def take(array, k):
        for p in range(PIECES):
            z_in(array, k, p).wait_recv()

            @pl.when(inner)
            def _():
                relay(array, k, p).start()

            x_copy(array, k, p).start()

    def wait_x(array, k):
        for p in range(PIECES):
            x_in(array, k, p).wait_recv()

    for p in range(PIECES):
        own_to_mate(T, p).start()
        x_copy(T, OWN, p).start()

    @pl.when(inner)
    def _():
        for p in range(PIECES):
            own_to_cross(T, p).start()

    label_copies = []
    for d in range(3):
        label_copies.append(remote(lab_ref, marks.at[z], sl.at[d], rl.at[d], {"ctx": peers[d]}))
        label_copies[-1].start()
    tok[z, :, mine] = tok_ref[...]
    grd[z, :, mine] = gro_ref[...]
    marks[z] = lab_ref[...]
    for copy in w_copies:
        copy.wait()

    def project(k):
        wait_x(T, k)
        here = block(places[k], count)
        tokens = tok[places[k]]
        for j in range(3):
            value = dot_general(tokens, w3_ref[j], 1, 0).astype(BF16)
            for h in range(4):
                qkv[j, h, here, :] = value[:, h * HD : (h + 1) * HD]

    def cotangents(k):
        wait_x(G, k)
        value = dot_general(grd[places[k]], wo_ref[...], 1, 1).astype(BF16)
        for h in range(4):
            cot[h, places[k]] = value[:, h * HD : (h + 1) * HD]

    def mask(h, k):
        columns = label_cols[h]
        return jnp.concatenate([columns] * (count // HD), axis=1) == label_rows[h, places[k]]

    def forward(k):
        here = block(places[k], count)

        @pl.loop(0, 2)
        def _(pair):
            for i in range(2):
                h = pair * 2 + i
                scores = dot_general(qkv[1, h], qkv[0, h, here, :], 1, 1) * (scale * LOG2E)
                scores = jnp.where(mask(h, k), scores, F32(-1e30))
                top = jnp.max(scores, axis=0, keepdims=True)
                expo = jnp.exp2(scores - top)
                total = jnp.sum(expo, axis=0, keepdims=True)
                probs = (expo * (1.0 / total)).astype(BF16)
                lse[h, places[k]] = top + jnp.log2(total)
                att[h, here, :] = dot_general(qkv[2, h], probs, 0, 0).T.astype(BF16)

    def backward(k, sums, first):
        here = block(places[k], count)

        @pl.loop(0, 2)
        def _(pair):
            for i in range(2):
                h = pair * 2 + i
                keys, values, query = qkv[1, h], qkv[2, h], qkv[0, h, here, :]
                cotangent = cot[h, places[k]]
                product = cotangent.astype(F32) * att[h, here, :].astype(F32)
                delta = jnp.sum(product.T, axis=0, keepdims=True)
                scores = dot_general(keys, query, 1, 1) * (scale * LOG2E) - lse[h, places[k]]
                probs = jnp.exp2(jnp.where(mask(h, k), scores, F32(-1e30)))
                grad_values = dot_general(probs.astype(BF16), cotangent, 1, 0)
                dprob = dot_general(values, cotangent, 1, 1)
                dscore = (probs * (dprob - delta) * scale).astype(BF16)
                grad_keys = dot_general(dscore, query, 1, 0)
                grads[0, h, here, :] = dot_general(keys, dscore, 0, 0).T.astype(BF16)
                if first:
                    sums[0, h] = grad_keys
                    sums[1, h] = grad_values
                else:
                    sums[0, h] += grad_keys
                    sums[1, h] += grad_values

    take(T, MATE)
    for p in range(PIECES):
        pl.when(jnp.logical_not(inner))(own_to_mate(G, p).start)
        pl.when(inner)(own_to_cross(G, p).start)
    project(OWN)
    take(T, NEXT)
    project(MATE)
    take(T, LAST)
    for p in range(PIECES):
        pl.when(inner)(own_to_mate(G, p).start)
        x_copy(G, OWN, p).start()
    for copy in label_copies:
        copy.wait_recv()
    for h in range(4):
        for b in range(4):
            row = marks[b, h : h + 1, :].astype(F32)
            label_rows[h, b] = row
            label_cols[h, b * count : (b + 1) * count, :] = jnp.broadcast_to(row, (HD, count)).T
    project(NEXT)
    take(G, MATE)
    project(LAST)
    forward(OWN)
    take(G, NEXT)
    forward(MATE)
    forward(NEXT)
    take(G, LAST)
    forward(LAST)

    t_copies = []

    def send_terms(t, term):
        x_send[t] = term(other_x).astype(BF16)
        t_copies.append(remote(x_send.at[t], x_recv.at[t], st.at[t], rt.at[t], x_dev))
        t_copies[-1].start()
        return term(x)

    def heads_of(ref, at):
        return jnp.concatenate([ref[h, at, :] for h in range(4)], axis=1)

    own_rows = block(z, count)

    def attended_term(f):
        return dot_general(heads_of(att, own_rows), wo_ref[:, block(f, half)], 1, 0)

    def token_term(f):
        total = None
        for j in range(3):
            term = dot_general(heads_of(grads.at[j], own_rows), w3_ref[j, block(f, half), :], 1, 1)
            total = term if total is None else total + term
        return total

    cotangents(OWN)
    backward(OWN, near, True)
    cotangents(MATE)
    backward(MATE, near, False)
    cotangents(NEXT)
    backward(NEXT, far, True)
    x_own = [send_terms(0, attended_term)]
    cotangents(LAST)
    backward(LAST, far, False)
    for h in range(4):
        for j in range(2):
            grads[1 + j, h] = (near[j, h] + far[j, h]).astype(BF16)
    x_own.append(send_terms(1, token_term))

    w_remote = []

    width = w3_ref.shape[1]
    everything = slice(None)
    all_tokens = tok[...].reshape(4 * count, width)
    for j in range(3):
        value = dot_general(all_tokens, heads_of(grads.at[j], everything), 0, 0)
        own_w[j] = value.astype(BF16)
        w_remote.append(remote(own_w.at[j], other_w.at[j], sw.at[j], rw.at[j], c_dev))
        w_remote[-1].start()
    all_grads = grd[...].reshape(4 * count, width)
    value = dot_general(heads_of(att, everything), all_grads, 0, 0)
    for f in range(2):
        own_w[3, f * half : (f + 1) * half, :] = value[:, f * half : (f + 1) * half].astype(BF16)
    w_remote.append(remote(own_w.at[3], other_w.at[3], sw.at[3], rw.at[3], c_dev))
    w_remote[-1].start()
    for j in range(3):
        w_remote[j].wait_recv()
        gwq_out[j] = own_w[j].astype(F32) + other_w[j].astype(F32)
    w_remote[3].wait_recv()
    for f in range(2):
        at = slice(f * half, (f + 1) * half)
        gwo_out[:, at] = own_w[3, at, :].astype(F32) + other_w[3, at, :].astype(F32)
    for t, target in ((0, att_out), (1, tokgrad_out)):
        t_copies[t].wait_recv()
        target[...] = (x_own[t] + x_recv[t].astype(F32)).astype(BF16)

    for copy in [*label_copies, *w_remote, *t_copies]:
        copy.wait_send()
    for array in (T, G):
        for p in range(PIECES):
            own_to_mate(array, p).wait_send()
            for k in range(4):
                x_copy(array, k, p).wait_send()

    @pl.when(inner)
    def _():
        for array in (T, G):
            for p in range(PIECES):
                own_to_cross(array, p).wait_send()
                for k in (MATE, NEXT, LAST):
                    relay(array, k, p).wait_send()


def whole_layer(tokens, w_qkv, w_out, labels, grad_out):
    count, half = tokens.shape[1:]
    width = w_qkv.shape[0]
    size = w_out.shape[0]
    any_spec = pl.BlockSpec(memory_space=pl.ANY)
    dma = pltpu.SemaphoreType.DMA
    scratch = [
        pltpu.VMEM((3, width, size), BF16),
        pltpu.VMEM((size, width), BF16),
        pltpu.VMEM((4, count, width), BF16),
        pltpu.VMEM((4, count, width), BF16),
        pltpu.VMEM((3, 4, 4 * count, HD), BF16),
        pltpu.VMEM((4, 4, count, HD), BF16),
        pltpu.VMEM((4, 4, count), jnp.int32),
        pltpu.VMEM((4, 4, 1, count), F32),
        pltpu.VMEM((4, 4 * count, HD), F32),
        pltpu.VMEM((4, 4, 1, count), F32),
        pltpu.VMEM((4, 4 * count, HD), BF16),
        pltpu.VMEM((2, 4, 4 * count, HD), F32),
        pltpu.VMEM((2, 4, 4 * count, HD), F32),
        pltpu.VMEM((3, 4, 4 * count, HD), BF16),
        pltpu.VMEM((4, width, size), BF16),
        pltpu.VMEM((4, width, size), BF16),
        pltpu.VMEM((2, count, half), BF16),
        pltpu.VMEM((2, count, half), BF16),
    ]
    for shape in ((2, 5, PIECES), (2, 4, PIECES), (2, 4, PIECES), (2, 4, PIECES), (3,), (3,), (4,), (4,), (2,), (2,), (2,)):
        scratch.append(dma(shape))
    attended, grad_tokens, grad_qkv, grad_w_out = pl.pallas_call(
        layer_kernel,
        out_shape=[
            pltpu.VMEM((count, half), BF16),
            pltpu.VMEM((count, half), BF16),
            pltpu.VMEM((3, width, size), F32),
            pltpu.VMEM((size, width), F32),
        ],
        in_specs=[VMEM_SPEC] * 2 + [any_spec] * 2 + [VMEM_SPEC],
        out_specs=[VMEM_SPEC] * 4,
        scratch_shapes=scratch,
        compiler_params=pltpu.CompilerParams(
            collective_id=0, has_side_effects=True, vmem_limit_bytes=50 * 2**20
        ),
    )(tokens[0], grad_out[0], jnp.transpose(w_qkv, (1, 0, 2)), w_out, labels[0])
    return attended[None], grad_tokens[None], jnp.transpose(grad_qkv, (1, 0, 2)), grad_w_out


VMEM_SPEC = pl.BlockSpec(memory_space=pltpu.VMEM)


def call(kernel, shapes, scratch=(), **kw):
    return pl.pallas_call(
        kernel,
        out_shape=[jax.ShapeDtypeStruct(s, t) for s, t in shapes],
        out_specs=[VMEM_SPEC] * len(shapes),
        scratch_shapes=list(scratch),
        compiler_params=pltpu.CompilerParams(vmem_limit_bytes=56 * 2**20),
        **kw,
    )


def shards(tokens, w_qkv, w_out, labels, grad_out):
    heads = w_out.shape[0] // HD
    ctx_count = lax.axis_size("ctx")
    if (
        ctx_count == 4
        and heads == 4
        and lax.axis_size("tensor") == 2
        and lax.axis_size("dp") == 2
        and tokens.shape[1:] == (256, 512)
    ):
        return whole_layer(tokens, w_qkv, w_out, labels, grad_out)
    repeat = ctx_count // heads
    inner = [[g * heads + i for i in range(heads)] for g in range(repeat)]
    outer = [[g * heads + i for g in range(repeat)] for i in range(heads)]
    width = w_qkv.shape[0]
    size = heads * HD
    w_flat = w_qkv.reshape(width, 3 * size)

    marks_all = lax.all_gather(labels[0], "ctx", axis=1, tiled=True)
    rows = lax.all_gather(tokens, "tensor", axis=2, tiled=True)[0]
    grads = lax.all_gather(grad_out, "tensor", axis=2, tiled=True)[0]
    count = rows.shape[0]

    (packed,) = call(project_kernel, [((heads, count, 4 * HD), BF16)], in_specs=[VMEM_SPEC] * 4)(
        rows, grads, w_flat, w_out
    )
    me = lax.axis_index("ctx")
    head_of = me % heads
    exchange = functools.partial(
        lax.all_to_all, axis_name="ctx", split_axis=0, concat_axis=0, tiled=True, axis_index_groups=inner
    )
    mine = exchange(packed).reshape(heads * count, 4 * HD)
    total = heads * count
    key_marks = lax.dynamic_slice_in_dim(marks_all, head_of, 1, 0)
    row_marks = lax.dynamic_slice_in_dim(key_marks, (me // heads) * total, total, 1).reshape(total, 1)
    key_total = total * repeat
    block_rows = 256
    acc = [pltpu.VMEM((key_total, HD), F32)] * 2 if total // block_rows > 4 else [pltpu.VMEM((8, HD), F32)] * 2
    if repeat == 1:
        (back,) = call(
            functools.partial(attention_kernel, True, block_rows),
            [((total, 4 * HD), BF16)],
            acc,
            in_specs=[VMEM_SPEC] * 4,
        )(mine, mine[:8, : 2 * HD], row_marks, key_marks)
    else:
        keys_values = lax.all_gather(
            mine[:, HD : 3 * HD], "ctx", axis=0, tiled=True, axis_index_groups=outer
        )
        back, terms = call(
            functools.partial(attention_kernel, False, block_rows),
            [((total, 4 * HD), BF16), ((key_total, 2 * HD), BF16)],
            acc,
            in_specs=[VMEM_SPEC] * 4,
        )(mine, keys_values, row_marks, key_marks)
        summed = lax.psum_scatter(
            terms, "ctx", scatter_dimension=0, tiled=True, axis_index_groups=outer
        )
        back = jnp.concatenate([back[:, :HD], summed, back[:, 3 * HD :]], axis=1)
    home = exchange(back.reshape(heads, count, 4 * HD))
    out_terms, in_terms, grad_w_qkv, grad_w_out = call(
        finish_kernel,
        [
            ((count, width), BF16),
            ((count, width), BF16),
            ((width, 3 * size), BF16),
            ((size, width), BF16),
        ],
        in_specs=[VMEM_SPEC] * 5,
    )(home, rows, grads, w_flat, w_out)
    summed_qkv = lax.psum(grad_w_qkv, ("ctx", "dp")).astype(F32).reshape(width, 3, size)
    summed_out = lax.psum(grad_w_out, ("ctx", "dp")).astype(F32)
    attended = lax.psum_scatter(out_terms, "tensor", scatter_dimension=1, tiled=True)
    grad_tokens = lax.psum_scatter(in_terms, "tensor", scatter_dimension=1, tiled=True)
    return (attended[None], grad_tokens[None], summed_qkv, summed_out)


def solution(mesh):
    placed = (
        P(("groups", "dp"), "ctx", "tensor"),
        P(None, None, "tensor"),
        P("tensor", None),
        P(("groups", "dp"), "tensor", "ctx"),
        P(("groups", "dp"), "ctx", "tensor"),
    )
    return jax.shard_map(
        shards,
        mesh=mesh,
        in_specs=placed,
        out_specs=(
            P(("groups", "dp"), "ctx", "tensor"),
            P(("groups", "dp"), "ctx", "tensor"),
            P("groups", None, "tensor"),
            P(("groups", "tensor"), None),
        ),
        check_vma=False,
    )
```

```python
import functools

import jax
import jax.numpy as jnp
from jax import lax
from jax.experimental import pallas as pl
from jax.experimental.pallas import tpu as pltpu
from jax.sharding import PartitionSpec as P

HD = 128
F32 = jnp.float32
BF16 = jnp.bfloat16


def dot_general(left, right, left_dim, right_dim):
    return lax.dot_general(
        left, right, (((left_dim,), (right_dim,)), ((), ())), preferred_element_type=F32
    )


def project_kernel(rows_ref, grads_ref, w_qkv_ref, w_out_ref, out_ref):
    heads = out_ref.shape[0]
    size = heads * HD
    for j in range(3):
        part = dot_general(rows_ref[...], w_qkv_ref[:, j * size : (j + 1) * size], 1, 0).astype(BF16)
        for h in range(heads):
            out_ref[h, :, j * HD : (j + 1) * HD] = part[:, h * HD : (h + 1) * HD]
    part = dot_general(grads_ref[...], w_out_ref[...], 1, 1).astype(BF16)
    for h in range(heads):
        out_ref[h, :, 3 * HD :] = part[:, h * HD : (h + 1) * HD]


def attention_kernel(own_keys, block_rows, x_ref, kv_ref, mark_ref, key_mark_ref, *outs):
    if own_keys:
        (y_ref, gk_acc, gv_acc) = outs
        keys = x_ref[:, HD : 2 * HD]
        values = x_ref[:, 2 * HD : 3 * HD]
    else:
        (y_ref, gkv_ref, gk_acc, gv_acc) = outs
        keys = kv_ref[:, :HD]
        values = kv_ref[:, HD:]
    key_marks = key_mark_ref[...]
    count = x_ref.shape[0] // block_rows

    def one_block(b):
        rows = pl.ds(pl.multiple_of(b * block_rows, block_rows), block_rows)
        query = x_ref[rows, :HD]
        cot = x_ref[rows, 3 * HD :]
        scores = dot_general(query, keys, 1, 1) * HD ** (-0.5)
        scores = jnp.where(mark_ref[rows, :] == key_marks, scores, F32(-1e30))
        top = jnp.max(scores, axis=1, keepdims=True)
        expo = jnp.exp(scores - top)
        full = expo * (1.0 / jnp.sum(expo, axis=1, keepdims=True))
        probs = full.astype(BF16)
        attention = dot_general(probs, values, 1, 0).astype(BF16)
        dprob = dot_general(cot, values, 1, 1)
        delta = jnp.sum(cot.astype(F32) * attention.astype(F32), axis=1, keepdims=True)
        dscore = (full * (dprob - delta) * HD ** (-0.5)).astype(BF16)
        y_ref[rows, :HD] = dot_general(dscore, keys, 1, 0).astype(BF16)
        y_ref[rows, 3 * HD :] = attention
        return dot_general(dscore, query, 0, 0), dot_general(probs, cot, 0, 0)

    if count <= 4:
        grad_keys, grad_values = one_block(0)
        for b in range(1, count):
            more_keys, more_values = one_block(b)
            grad_keys = grad_keys + more_keys
            grad_values = grad_values + more_values
    else:
        gk_acc[...] = jnp.zeros_like(gk_acc)
        gv_acc[...] = jnp.zeros_like(gv_acc)

        @pl.loop(0, count)
        def _(b):
            more_keys, more_values = one_block(b)
            gk_acc[...] += more_keys
            gv_acc[...] += more_values

        grad_keys, grad_values = gk_acc[...], gv_acc[...]
    if own_keys:
        y_ref[:, HD : 2 * HD] = grad_keys.astype(BF16)
        y_ref[:, 2 * HD : 3 * HD] = grad_values.astype(BF16)
    else:
        gkv_ref[:, :HD] = grad_keys.astype(BF16)
        gkv_ref[:, HD:] = grad_values.astype(BF16)


def finish_kernel(z_ref, rows_ref, grads_ref, w_qkv_ref, w_out_ref, out_ref, in_ref, gwq_ref, gwo_ref):
    heads = z_ref.shape[0]
    size = heads * HD
    attention = jnp.concatenate([z_ref[h, :, 3 * HD :] for h in range(heads)], axis=1)
    out_ref[...] = dot_general(attention, w_out_ref[...], 1, 0).astype(BF16)
    gwo_ref[...] = dot_general(attention, grads_ref[...], 0, 0).astype(BF16)
    total = None
    for j in range(3):
        grad = jnp.concatenate([z_ref[h, :, j * HD : (j + 1) * HD] for h in range(heads)], axis=1)
        cols = slice(j * size, (j + 1) * size)
        term = dot_general(grad, w_qkv_ref[:, cols], 1, 1)
        total = term if total is None else total + term
        gwq_ref[:, cols] = dot_general(rows_ref[...], grad, 0, 0).astype(BF16)
    in_ref[...] = total.astype(BF16)


def remote(source, target, send_sem, recv_sem, device):
    return pltpu.make_async_remote_copy(
        src_ref=source,
        dst_ref=target,
        send_sem=send_sem,
        recv_sem=recv_sem,
        device_id=device,
        device_id_type=pl.DeviceIdType.MESH,
    )


LOG2E = 1.4426950408889634
PIECES = 2


def layer_kernel(
    tok_ref, gro_ref, w3_hbm, wo_hbm, lab_ref,
    att_out, tokgrad_out, own_w, other_w,
    w3_ref, wo_ref, tok, grd, qkv, cot, marks, label_rows, label_cols, probs_full, att,
    near, far, grads, x_send, x_recv,
    sz, rz, sx, rx, sl, rl, sw, rw, st, rt, wsem,
):
    z = lax.axis_index("ctx")
    x = lax.axis_index("tensor")
    c = lax.axis_index("dp")
    count, half = tok_ref.shape
    scale = HD ** (-0.5)
    other_x = 1 - x
    x_dev = {"tensor": other_x}
    c_dev = {"dp": 1 - c}
    peers = [lax.rem(z + d, 4) for d in range(1, 4)]
    side = z // 2
    mate = z + 1 - 2 * (z % 2)
    inner = jnp.logical_or(z == 1, z == 2)
    cross_dev = {"ctx": 3 - z}
    mate_dev = {"ctx": mate}
    places = (z, mate, 2 - side, 3 - 3 * side)
    OWN, MATE, NEXT, LAST = range(4)

    w_copies = [
        pltpu.make_async_copy(w3_hbm, w3_ref, wsem.at[0]),
        pltpu.make_async_copy(wo_hbm, wo_ref, wsem.at[1]),
    ]
    for copy in w_copies:
        copy.start()
    barrier = pltpu.get_barrier_semaphore()
    for device in [{"ctx": p} for p in peers] + [x_dev, c_dev]:
        pl.semaphore_signal(barrier, inc=1, device_id=device, device_id_type=pl.DeviceIdType.MESH)
    pl.semaphore_wait(barrier, 5)

    def block(index, size):
        return pl.ds(pl.multiple_of(index * size, size), size)

    piece = count // PIECES
    inputs = (tok_ref, gro_ref)
    gathered = (tok, grd)
    T, G = 0, 1
    mine = block(x, half)

    def rows(p):
        return slice(p * piece, (p + 1) * piece)

    def home(array, k, p):
        return gathered[array].at[places[k], rows(p), mine]

    def z_copy(array, k, p, slot, route, device):
        source = inputs[array].at[rows(p)] if k == OWN else home(array, k, p)
        return remote(source, home(array, k, p), sz.at[array, route, p], rz.at[array, slot, p], device)

    def z_in(array, k, p):
        return remote(home(array, k, p), home(array, k, p), sz.at[array, 0, p], rz.at[array, k, p], mate_dev)

    def x_copy(array, k, p):
        source = inputs[array].at[rows(p)] if k == OWN else home(array, k, p)
        return remote(source, home(array, k, p), sx.at[array, k, p], rx.at[array, k, p], x_dev)

    def x_in(array, k, p):
        there = gathered[array].at[places[k], rows(p), block(other_x, half)]
        return remote(there, there, sx.at[array, k, p], rx.at[array, k, p], x_dev)

    def own_to_mate(array, p):
        return z_copy(array, OWN, p, MATE, 0, mate_dev)

    def own_to_cross(array, p):
        return z_copy(array, OWN, p, NEXT, 1, cross_dev)

    def relay(array, k, p):
        if k == MATE:
            return z_copy(array, MATE, p, LAST, 2, cross_dev)
        return z_copy(array, k, p, k, k + 1, mate_dev)

    def across(p):
        there = grd.at[z, rows(p), block(other_x, half)]
        return remote(there, there, sz.at[G, 5, p], rz.at[G, OWN, p], mate_dev)

    def across_in(p):
        there = grd.at[mate, rows(p), block(other_x, half)]
        return remote(there, there, sz.at[G, 5, p], rz.at[G, OWN, p], mate_dev)

    def take_inner(array, k, p):
        @pl.when(inner)
        def _():
            z_in(array, k, p).wait_recv()
            relay(array, k, p).start()
            if (array, k) != (G, MATE):
                x_copy(array, k, p).start()

    def take_outer(array, k, p):
        @pl.when(jnp.logical_not(inner))
        def _():
            z_in(array, k, p).wait_recv()
            if (array, k) != (G, MATE):
                x_copy(array, k, p).start()

    def wait_x(array, k):
        for p in range(PIECES):
            if (array, k) == (G, MATE):
                across_in(p).wait_recv()
            else:
                x_in(array, k, p).wait_recv()

    for p in range(PIECES):
        own_to_mate(T, p).start()
        x_copy(T, OWN, p).start()

    @pl.when(inner)
    def _():
        for p in range(PIECES):
            own_to_cross(T, p).start()

    label_copies = []
    for d in range(3):
        label_copies.append(remote(lab_ref, marks.at[z], sl.at[d], rl.at[d], {"ctx": peers[d]}))
        label_copies[-1].start()
    tok[z, :, mine] = tok_ref[...]
    grd[z, :, mine] = gro_ref[...]
    marks[z] = lab_ref[...]
    for copy in w_copies:
        copy.wait()

    def project(k):
        here = block(places[k], count)
        tokens = tok[places[k]]
        for j in range(3):
            value = dot_general(tokens, w3_ref[j], 1, 0).astype(BF16)
            for h in range(4):
                qkv[j, h, here, :] = value[:, h * HD : (h + 1) * HD]

    def cotangents(k):
        value = dot_general(grd[places[k]], wo_ref[...], 1, 1).astype(BF16)
        for h in range(4):
            cot[h, places[k]] = value[:, h * HD : (h + 1) * HD]

    def mask(h, k):
        columns = label_cols[h]
        return jnp.concatenate([columns] * (count // HD), axis=1) == label_rows[h, places[k]]

    def reduce_rows(array, op):
        parts = array.reshape(8, array.shape[0] // 8, array.shape[1])
        return op(op(parts, axis=0), axis=0, keepdims=True)

    def forward(k):
        here = block(places[k], count)
        for h in range(4):
            scores = dot_general(qkv[1, h], qkv[0, h, here, :], 1, 1) * (scale * LOG2E)
            scores = jnp.where(mask(h, k), scores, F32(-1e30))
            expo = jnp.exp2(scores - reduce_rows(scores, jnp.max))
            probs = expo * (1.0 / reduce_rows(expo, jnp.sum))
            probs_full[h, k] = probs
            att[h, here, :] = dot_general(probs.astype(BF16), qkv[2, h], 0, 0).astype(BF16)

    def backward(k, sums, first):
        here = block(places[k], count)
        for h in range(4):
            keys, values, query = qkv[1, h], qkv[2, h], qkv[0, h, here, :]
            cotangent = cot[h, places[k]]
            product = cotangent.astype(F32) * att[h, here, :].astype(F32)
            delta = jnp.sum(product.T, axis=0, keepdims=True)
            probs = probs_full[h, k]
            grad_values = dot_general(probs.astype(BF16), cotangent, 1, 0)
            dprob = dot_general(values, cotangent, 1, 1)
            dscore = (probs * (dprob - delta) * scale).astype(BF16)
            grad_keys = dot_general(dscore, query, 1, 0)
            grads[0, h, here, :] = dot_general(keys, dscore, 0, 0).T.astype(BF16)
            if first:
                sums[0, h] = grad_keys
                sums[1, h] = grad_values
            else:
                sums[0, h] += grad_keys
                sums[1, h] += grad_values

    for p in range(PIECES):
        take_outer(T, MATE, p)
        take_inner(T, MATE, p)
    for p in range(PIECES):
        take_inner(T, NEXT, p)
        pl.when(jnp.logical_not(inner))(own_to_mate(G, p).start)
        pl.when(inner)(own_to_cross(G, p).start)
    wait_x(T, OWN)
    project(OWN)
    for p in range(PIECES):
        take_outer(T, NEXT, p)
        take_inner(T, LAST, p)
    for p in range(PIECES):
        pl.when(inner)(own_to_mate(G, p).start)
        pl.when(inner)(x_copy(G, OWN, p).start)
    wait_x(T, MATE)
    project(MATE)
    for p in range(PIECES):
        take_inner(G, MATE, p)
    for copy in label_copies:
        copy.wait_recv()
    for h in range(4):
        for b in range(4):
            row = marks[b, h : h + 1, :].astype(F32)
            label_rows[h, b] = row
            label_cols[h, b * count : (b + 1) * count, :] = jnp.broadcast_to(row, (HD, count)).T
    for p in range(PIECES):
        take_outer(T, LAST, p)
        take_inner(G, NEXT, p)
    for p in range(PIECES):
        pl.when(jnp.logical_not(inner))(x_copy(G, OWN, p).start)
    wait_x(T, NEXT)
    project(NEXT)
    for p in range(PIECES):
        take_inner(G, LAST, p)
    wait_x(T, LAST)
    project(LAST)
    forward(OWN)
    for p in range(PIECES // 2):
        take_outer(G, NEXT, p)
    forward(MATE)
    for p in range(PIECES // 2, PIECES):
        take_outer(G, NEXT, p)
    forward(NEXT)
    for p in range(PIECES):
        x_in(G, OWN, p).wait_recv()
        across(p).start()
    for p in range(PIECES // 2):
        take_outer(G, LAST, p)
    forward(LAST)
    for p in range(PIECES // 2, PIECES):
        take_outer(G, LAST, p)
    for p in range(PIECES):
        take_outer(G, MATE, p)

    t_copies = []

    def send_terms(t, term):
        x_send[t] = term(other_x).astype(BF16)
        t_copies.append(remote(x_send.at[t], x_recv.at[t], st.at[t], rt.at[t], x_dev))
        t_copies[-1].start()
        return term(x)

    def heads_of(ref, at):
        return jnp.concatenate([ref[h, at, :] for h in range(4)], axis=1)

    own_rows = block(z, count)

    def attended_term(f):
        return dot_general(heads_of(att, own_rows), wo_ref[:, block(f, half)], 1, 0)

    def token_term(f):
        total = None
        for j in range(3):
            term = dot_general(heads_of(grads.at[j], own_rows), w3_ref[j, block(f, half), :], 1, 1)
            total = term if total is None else total + term
        return total

    x_own = [send_terms(0, attended_term)]
    cotangents(OWN)
    backward(OWN, near, True)
    wait_x(G, NEXT)
    cotangents(NEXT)
    backward(NEXT, far, True)
    wait_x(G, MATE)
    cotangents(MATE)
    backward(MATE, near, False)
    wait_x(G, LAST)
    cotangents(LAST)
    backward(LAST, far, False)
    for h in range(4):
        for j in range(2):
            grads[1 + j, h] = (near[j, h] + far[j, h]).astype(BF16)
    x_own.append(send_terms(1, token_term))

    w_remote = []

    width = w3_ref.shape[1]
    everything = slice(None)
    all_tokens = tok[...].reshape(4 * count, width)
    for j in range(3):
        value = dot_general(all_tokens, heads_of(grads.at[j], everything), 0, 0)
        own_w[j] = value.astype(BF16)
        w_remote.append(remote(own_w.at[j], other_w.at[j], sw.at[j], rw.at[j], c_dev))
        w_remote[-1].start()
    all_grads = grd[...].reshape(4 * count, width)
    value = dot_general(heads_of(att, everything), all_grads, 0, 0)
    for f in range(2):
        own_w[3, f * half : (f + 1) * half, :] = value[:, f * half : (f + 1) * half].astype(BF16)
    w_remote.append(remote(own_w.at[3], other_w.at[3], sw.at[3], rw.at[3], c_dev))
    w_remote[-1].start()
    for copy in w_remote:
        copy.wait_recv()
    for t, target in ((0, att_out), (1, tokgrad_out)):
        t_copies[t].wait_recv()
        target[...] = (x_own[t] + x_recv[t].astype(F32)).astype(BF16)

    for copy in [*label_copies, *w_remote, *t_copies]:
        copy.wait_send()
    for array in (T, G):
        for p in range(PIECES):
            own_to_mate(array, p).wait_send()
            for k in range(4):
                if (array, k) != (G, MATE):
                    x_copy(array, k, p).wait_send()
    for p in range(PIECES):
        across(p).wait_send()

    @pl.when(inner)
    def _():
        for array in (T, G):
            for p in range(PIECES):
                own_to_cross(array, p).wait_send()
                for k in (MATE, NEXT, LAST):
                    relay(array, k, p).wait_send()


def finish_sums(att_ref, tokgrad_ref, own_ref, other_ref, att_out, tokgrad_out, gwq_out, gwo_out, stage, sem):
    half = own_ref.shape[2]
    copies = [
        pltpu.make_async_copy(att_ref, att_out, sem.at[4]),
        pltpu.make_async_copy(tokgrad_ref, tokgrad_out, sem.at[5]),
    ]
    for u in range(4):
        if u < 3:
            stage[u] = own_ref[u].astype(F32) + other_ref[u].astype(F32)
            copies.append(pltpu.make_async_copy(stage.at[u], gwq_out.at[u], sem.at[u]))
        else:
            for f in range(2):
                at = slice(f * half, (f + 1) * half)
                stage[u, at, :] = own_ref[u, at, :].astype(F32) + other_ref[u, at, :].astype(F32)
                copies.append(pltpu.make_async_copy(stage.at[u, at], gwo_out.at[:, at], sem.at[(u, 6)[f]]))
                if f == 0:
                    copies[-1].start()
        if u == 0:
            copies[0].start()
            copies[1].start()
        copies[-1].start()
    for copy in copies:
        copy.wait()


def whole_layer(tokens, w_qkv, w_out, labels, grad_out):
    count, half = tokens.shape[1:]
    width = w_qkv.shape[0]
    size = w_out.shape[0]
    any_spec = pl.BlockSpec(memory_space=pl.ANY)
    dma = pltpu.SemaphoreType.DMA
    scratch = [
        pltpu.VMEM((3, width, size), BF16),
        pltpu.VMEM((size, width), BF16),
        pltpu.VMEM((4, count, width), BF16),
        pltpu.VMEM((4, count, width), BF16),
        pltpu.VMEM((3, 4, 4 * count, HD), BF16),
        pltpu.VMEM((4, 4, count, HD), BF16),
        pltpu.VMEM((4, 4, count), jnp.int32),
        pltpu.VMEM((4, 4, 1, count), F32),
        pltpu.VMEM((4, 4 * count, HD), F32),
        pltpu.VMEM((4, 4, 4 * count, count), F32),
        pltpu.VMEM((4, 4 * count, HD), BF16),
        pltpu.VMEM((2, 4, 4 * count, HD), F32),
        pltpu.VMEM((2, 4, 4 * count, HD), F32),
        pltpu.VMEM((3, 4, 4 * count, HD), BF16),
        pltpu.VMEM((2, count, half), BF16),
        pltpu.VMEM((2, count, half), BF16),
    ]
    for shape in ((2, 6, PIECES), (2, 4, PIECES), (2, 4, PIECES), (2, 4, PIECES), (3,), (3,), (4,), (4,), (2,), (2,), (2,)):
        scratch.append(dma(shape))
    partial = pl.pallas_call(
        layer_kernel,
        out_shape=[
            pltpu.VMEM((count, half), BF16),
            pltpu.VMEM((count, half), BF16),
            pltpu.VMEM((4, width, size), BF16),
            pltpu.VMEM((4, width, size), BF16),
        ],
        in_specs=[VMEM_SPEC] * 2 + [any_spec] * 2 + [VMEM_SPEC],
        out_specs=[VMEM_SPEC] * 4,
        scratch_shapes=scratch,
        compiler_params=pltpu.CompilerParams(
            collective_id=0, has_side_effects=True, vmem_limit_bytes=54 * 2**20
        ),
    )(tokens[0], grad_out[0], jnp.transpose(w_qkv, (1, 0, 2)), w_out, labels[0])
    attended, grad_tokens, grad_qkv, grad_w_out = pl.pallas_call(
        finish_sums,
        out_shape=[
            jax.ShapeDtypeStruct((count, half), BF16),
            jax.ShapeDtypeStruct((count, half), BF16),
            jax.ShapeDtypeStruct((3, width, size), F32),
            jax.ShapeDtypeStruct((size, width), F32),
        ],
        in_specs=[VMEM_SPEC] * 4,
        out_specs=[any_spec] * 4,
        scratch_shapes=[pltpu.VMEM((4, width, size), F32), dma((7,))],
        compiler_params=pltpu.CompilerParams(vmem_limit_bytes=24 * 2**20),
    )(*partial)
    return attended[None], grad_tokens[None], jnp.transpose(grad_qkv, (1, 0, 2)), grad_w_out


VMEM_SPEC = pl.BlockSpec(memory_space=pltpu.VMEM)


def call(kernel, shapes, scratch=(), **kw):
    return pl.pallas_call(
        kernel,
        out_shape=[jax.ShapeDtypeStruct(s, t) for s, t in shapes],
        out_specs=[VMEM_SPEC] * len(shapes),
        scratch_shapes=list(scratch),
        compiler_params=pltpu.CompilerParams(vmem_limit_bytes=56 * 2**20),
        **kw,
    )


def shards(tokens, w_qkv, w_out, labels, grad_out):
    heads = w_out.shape[0] // HD
    ctx_count = lax.axis_size("ctx")
    if (
        ctx_count == 4
        and heads == 4
        and lax.axis_size("tensor") == 2
        and lax.axis_size("dp") == 2
        and tokens.shape[1:] == (256, 512)
    ):
        return whole_layer(tokens, w_qkv, w_out, labels, grad_out)
    repeat = ctx_count // heads
    inner = [[g * heads + i for i in range(heads)] for g in range(repeat)]
    outer = [[g * heads + i for g in range(repeat)] for i in range(heads)]
    width = w_qkv.shape[0]
    size = heads * HD
    w_flat = w_qkv.reshape(width, 3 * size)

    marks_all = lax.all_gather(labels[0], "ctx", axis=1, tiled=True)
    rows = lax.all_gather(tokens, "tensor", axis=2, tiled=True)[0]
    grads = lax.all_gather(grad_out, "tensor", axis=2, tiled=True)[0]
    count = rows.shape[0]

    (packed,) = call(project_kernel, [((heads, count, 4 * HD), BF16)], in_specs=[VMEM_SPEC] * 4)(
        rows, grads, w_flat, w_out
    )
    me = lax.axis_index("ctx")
    head_of = me % heads
    exchange = functools.partial(
        lax.all_to_all, axis_name="ctx", split_axis=0, concat_axis=0, tiled=True, axis_index_groups=inner
    )
    mine = exchange(packed).reshape(heads * count, 4 * HD)
    total = heads * count
    key_marks = lax.dynamic_slice_in_dim(marks_all, head_of, 1, 0)
    row_marks = lax.dynamic_slice_in_dim(key_marks, (me // heads) * total, total, 1).reshape(total, 1)
    key_total = total * repeat
    block_rows = 256
    acc = [pltpu.VMEM((key_total, HD), F32)] * 2 if total // block_rows > 4 else [pltpu.VMEM((8, HD), F32)] * 2
    if repeat == 1:
        (back,) = call(
            functools.partial(attention_kernel, True, block_rows),
            [((total, 4 * HD), BF16)],
            acc,
            in_specs=[VMEM_SPEC] * 4,
        )(mine, mine[:8, : 2 * HD], row_marks, key_marks)
    else:
        keys_values = lax.all_gather(
            mine[:, HD : 3 * HD], "ctx", axis=0, tiled=True, axis_index_groups=outer
        )
        back, terms = call(
            functools.partial(attention_kernel, False, block_rows),
            [((total, 4 * HD), BF16), ((key_total, 2 * HD), BF16)],
            acc,
            in_specs=[VMEM_SPEC] * 4,
        )(mine, keys_values, row_marks, key_marks)
        summed = lax.psum_scatter(
            terms, "ctx", scatter_dimension=0, tiled=True, axis_index_groups=outer
        )
        back = jnp.concatenate([back[:, :HD], summed, back[:, 3 * HD :]], axis=1)
    home = exchange(back.reshape(heads, count, 4 * HD))
    out_terms, in_terms, grad_w_qkv, grad_w_out = call(
        finish_kernel,
        [
            ((count, width), BF16),
            ((count, width), BF16),
            ((width, 3 * size), BF16),
            ((size, width), BF16),
        ],
        in_specs=[VMEM_SPEC] * 5,
    )(home, rows, grads, w_flat, w_out)
    summed_qkv = lax.psum(grad_w_qkv, ("ctx", "dp")).astype(F32).reshape(width, 3, size)
    summed_out = lax.psum(grad_w_out, ("ctx", "dp")).astype(F32)
    attended = lax.psum_scatter(out_terms, "tensor", scatter_dimension=1, tiled=True)
    grad_tokens = lax.psum_scatter(in_terms, "tensor", scatter_dimension=1, tiled=True)
    return (attended[None], grad_tokens[None], summed_qkv, summed_out)


def solution(mesh):
    placed = (
        P(("groups", "dp"), "ctx", "tensor"),
        P(None, None, "tensor"),
        P("tensor", None),
        P(("groups", "dp"), "tensor", "ctx"),
        P(("groups", "dp"), "ctx", "tensor"),
    )
    return jax.shard_map(
        shards,
        mesh=mesh,
        in_specs=placed,
        out_specs=(
            P(("groups", "dp"), "ctx", "tensor"),
            P(("groups", "dp"), "ctx", "tensor"),
            P("groups", None, "tensor"),
            P(("groups", "tensor"), None),
        ),
        check_vma=False,
    )
```

```python
import functools

import jax
import jax.numpy as jnp
from jax import lax
from jax.experimental import pallas as pl
from jax.experimental.pallas import tpu as pltpu
from jax.sharding import PartitionSpec as P

HD = 128
F32 = jnp.float32
BF16 = jnp.bfloat16


def dot_general(left, right, left_dim, right_dim):
    return lax.dot_general(
        left, right, (((left_dim,), (right_dim,)), ((), ())), preferred_element_type=F32
    )


def project_kernel(rows_ref, grads_ref, w_qkv_ref, w_out_ref, out_ref):
    heads = out_ref.shape[0]
    size = heads * HD
    for j in range(3):
        part = dot_general(rows_ref[...], w_qkv_ref[:, j * size : (j + 1) * size], 1, 0).astype(BF16)
        for h in range(heads):
            out_ref[h, :, j * HD : (j + 1) * HD] = part[:, h * HD : (h + 1) * HD]
    part = dot_general(grads_ref[...], w_out_ref[...], 1, 1).astype(BF16)
    for h in range(heads):
        out_ref[h, :, 3 * HD :] = part[:, h * HD : (h + 1) * HD]


def attention_kernel(own_keys, block_rows, x_ref, kv_ref, mark_ref, key_mark_ref, *outs):
    if own_keys:
        (y_ref, gk_acc, gv_acc) = outs
        keys = x_ref[:, HD : 2 * HD]
        values = x_ref[:, 2 * HD : 3 * HD]
    else:
        (y_ref, gkv_ref, gk_acc, gv_acc) = outs
        keys = kv_ref[:, :HD]
        values = kv_ref[:, HD:]
    key_marks = key_mark_ref[...]
    count = x_ref.shape[0] // block_rows

    def one_block(b):
        rows = pl.ds(pl.multiple_of(b * block_rows, block_rows), block_rows)
        query = x_ref[rows, :HD]
        cot = x_ref[rows, 3 * HD :]
        scores = dot_general(query, keys, 1, 1) * HD ** (-0.5)
        scores = jnp.where(mark_ref[rows, :] == key_marks, scores, F32(-1e30))
        top = jnp.max(scores, axis=1, keepdims=True)
        expo = jnp.exp(scores - top)
        full = expo * (1.0 / jnp.sum(expo, axis=1, keepdims=True))
        probs = full.astype(BF16)
        attention = dot_general(probs, values, 1, 0).astype(BF16)
        dprob = dot_general(cot, values, 1, 1)
        delta = jnp.sum(cot.astype(F32) * attention.astype(F32), axis=1, keepdims=True)
        dscore = (full * (dprob - delta) * HD ** (-0.5)).astype(BF16)
        y_ref[rows, :HD] = dot_general(dscore, keys, 1, 0).astype(BF16)
        y_ref[rows, 3 * HD :] = attention
        return dot_general(dscore, query, 0, 0), dot_general(probs, cot, 0, 0)

    if count <= 4:
        grad_keys, grad_values = one_block(0)
        for b in range(1, count):
            more_keys, more_values = one_block(b)
            grad_keys = grad_keys + more_keys
            grad_values = grad_values + more_values
    else:
        gk_acc[...] = jnp.zeros_like(gk_acc)
        gv_acc[...] = jnp.zeros_like(gv_acc)

        @pl.loop(0, count)
        def _(b):
            more_keys, more_values = one_block(b)
            gk_acc[...] += more_keys
            gv_acc[...] += more_values

        grad_keys, grad_values = gk_acc[...], gv_acc[...]
    if own_keys:
        y_ref[:, HD : 2 * HD] = grad_keys.astype(BF16)
        y_ref[:, 2 * HD : 3 * HD] = grad_values.astype(BF16)
    else:
        gkv_ref[:, :HD] = grad_keys.astype(BF16)
        gkv_ref[:, HD:] = grad_values.astype(BF16)


def finish_kernel(z_ref, rows_ref, grads_ref, w_qkv_ref, w_out_ref, out_ref, in_ref, gwq_ref, gwo_ref):
    heads = z_ref.shape[0]
    size = heads * HD
    attention = jnp.concatenate([z_ref[h, :, 3 * HD :] for h in range(heads)], axis=1)
    out_ref[...] = dot_general(attention, w_out_ref[...], 1, 0).astype(BF16)
    gwo_ref[...] = dot_general(attention, grads_ref[...], 0, 0).astype(BF16)
    total = None
    for j in range(3):
        grad = jnp.concatenate([z_ref[h, :, j * HD : (j + 1) * HD] for h in range(heads)], axis=1)
        cols = slice(j * size, (j + 1) * size)
        term = dot_general(grad, w_qkv_ref[:, cols], 1, 1)
        total = term if total is None else total + term
        gwq_ref[:, cols] = dot_general(rows_ref[...], grad, 0, 0).astype(BF16)
    in_ref[...] = total.astype(BF16)


def remote(source, target, send_sem, recv_sem, device):
    return pltpu.make_async_remote_copy(
        src_ref=source,
        dst_ref=target,
        send_sem=send_sem,
        recv_sem=recv_sem,
        device_id=device,
        device_id_type=pl.DeviceIdType.MESH,
    )


LOG2E = 1.4426950408889634
PIECES = 2


def layer_kernel(
    tok_ref, gro_ref, w3_hbm, wo_hbm, lab_ref,
    att_out, tokgrad_out, own_w, other_w,
    w3_ref, wo_ref, tok, grd, qkv, cot, marks, label_rows, label_cols, probs_full, att,
    near, far, grads, x_send, x_recv,
    sz, rz, sx, rx, sl, rl, sw, rw, st, rt, wsem,
):
    z = lax.axis_index("ctx")
    x = lax.axis_index("tensor")
    c = lax.axis_index("dp")
    count, half = tok_ref.shape
    scale = HD ** (-0.5)
    other_x = 1 - x
    x_dev = {"tensor": other_x}
    c_dev = {"dp": 1 - c}
    peers = [lax.rem(z + d, 4) for d in range(1, 4)]
    side = z // 2
    mate = z + 1 - 2 * (z % 2)
    inner = jnp.logical_or(z == 1, z == 2)
    cross_dev = {"ctx": 3 - z}
    mate_dev = {"ctx": mate}
    places = (z, mate, 2 - side, 3 - 3 * side)
    OWN, MATE, NEXT, LAST = range(4)

    barrier = pltpu.get_barrier_semaphore()
    for device in [{"ctx": p} for p in peers] + [x_dev, c_dev]:
        pl.semaphore_signal(barrier, inc=1, device_id=device, device_id_type=pl.DeviceIdType.MESH)

    def block(index, size):
        return pl.ds(pl.multiple_of(index * size, size), size)

    local_copies = [
        pltpu.make_async_copy(w3_hbm, w3_ref, wsem.at[0]),
        pltpu.make_async_copy(wo_hbm, wo_ref, wsem.at[1]),
        pltpu.make_async_copy(tok_ref, tok.at[z, :, block(x, half)], wsem.at[2]),
        pltpu.make_async_copy(gro_ref, grd.at[z, :, block(x, half)], wsem.at[3]),
    ]
    for copy in local_copies:
        copy.start()
    pl.semaphore_wait(barrier, 5)

    piece = count // PIECES
    inputs = (tok_ref, gro_ref)
    gathered = (tok, grd)
    T, G = 0, 1
    mine = block(x, half)

    def rows(p):
        return slice(p * piece, (p + 1) * piece)

    def home(array, k, p):
        return gathered[array].at[places[k], rows(p), mine]

    def z_copy(array, k, p, slot, route, device):
        source = inputs[array].at[rows(p)] if k == OWN else home(array, k, p)
        return remote(source, home(array, k, p), sz.at[array, route, p], rz.at[array, slot, p], device)

    def z_in(array, k, p):
        return remote(home(array, k, p), home(array, k, p), sz.at[array, 0, p], rz.at[array, k, p], mate_dev)

    def x_copy(array, k, p):
        source = inputs[array].at[rows(p)] if k == OWN else home(array, k, p)
        return remote(source, home(array, k, p), sx.at[array, k, p], rx.at[array, k, p], x_dev)

    def x_in(array, k, p):
        there = gathered[array].at[places[k], rows(p), block(other_x, half)]
        return remote(there, there, sx.at[array, k, p], rx.at[array, k, p], x_dev)

    def own_to_mate(array, p):
        return z_copy(array, OWN, p, MATE, 0, mate_dev)

    def own_to_cross(array, p):
        return z_copy(array, OWN, p, NEXT, 1, cross_dev)

    def relay(array, k, p):
        if k == MATE:
            return z_copy(array, MATE, p, LAST, 2, cross_dev)
        return z_copy(array, k, p, k, k + 1, mate_dev)

    def across(p):
        there = grd.at[z, rows(p), block(other_x, half)]
        return remote(there, there, sz.at[G, 5, p], rz.at[G, OWN, p], mate_dev)

    def across_in(p):
        there = grd.at[mate, rows(p), block(other_x, half)]
        return remote(there, there, sz.at[G, 5, p], rz.at[G, OWN, p], mate_dev)

    def take_inner(array, k, p):
        @pl.when(inner)
        def _():
            z_in(array, k, p).wait_recv()
            relay(array, k, p).start()
            if (array, k) != (G, MATE):
                x_copy(array, k, p).start()

    def take_outer(array, k, p):
        @pl.when(jnp.logical_not(inner))
        def _():
            z_in(array, k, p).wait_recv()
            if (array, k) != (G, MATE):
                x_copy(array, k, p).start()

    def wait_x(array, k):
        for p in range(PIECES):
            if (array, k) == (G, MATE):
                across_in(p).wait_recv()
            else:
                x_in(array, k, p).wait_recv()

    for p in range(PIECES):
        own_to_mate(T, p).start()
        x_copy(T, OWN, p).start()

    @pl.when(inner)
    def _():
        for p in range(PIECES):
            own_to_cross(T, p).start()

    label_copies = []
    for d in range(3):
        label_copies.append(remote(lab_ref, marks.at[z], sl.at[d], rl.at[d], {"ctx": peers[d]}))
        label_copies[-1].start()
    marks[z] = lab_ref[...]
    for copy in local_copies:
        copy.wait()

    def project(k):
        here = block(places[k], count)
        tokens = tok[places[k]]
        for j in range(3):
            value = dot_general(tokens, w3_ref[j], 1, 0).astype(BF16)
            for h in range(4):
                qkv[j, h, here, :] = value[:, h * HD : (h + 1) * HD]

    def cotangents(k):
        value = dot_general(grd[places[k]], wo_ref[...], 1, 1).astype(BF16)
        for h in range(4):
            cot[h, places[k]] = value[:, h * HD : (h + 1) * HD]

    def mask(h, k):
        columns = label_cols[h]
        return jnp.concatenate([columns] * (count // HD), axis=1) == label_rows[h, places[k]]

    def reduce_rows(array, op):
        parts = array.reshape(8, array.shape[0] // 8, array.shape[1])
        return op(op(parts, axis=0), axis=0, keepdims=True)

    def forward(k):
        here = block(places[k], count)
        for h in range(4):
            scores = dot_general(qkv[1, h], qkv[0, h, here, :], 1, 1) * (scale * LOG2E)
            scores = jnp.where(mask(h, k), scores, F32(-1e30))
            expo = jnp.exp2(scores - reduce_rows(scores, jnp.max))
            probs = expo * (1.0 / reduce_rows(expo, jnp.sum))
            probs_full[h, k] = probs
            att[h, here, :] = dot_general(probs.astype(BF16), qkv[2, h], 0, 0).astype(BF16)

    def backward(k, sums, first, final=False):
        here = block(places[k], count)
        for h in range(4):
            keys, values, query = qkv[1, h], qkv[2, h], qkv[0, h, here, :]
            cotangent = cot[h, places[k]]
            product = cotangent.astype(F32) * att[h, here, :].astype(F32)
            delta = jnp.sum(product.T, axis=0, keepdims=True)
            probs = probs_full[h, k]
            grad_values = dot_general(probs.astype(BF16), cotangent, 1, 0)
            dprob = dot_general(values, cotangent, 1, 1)
            dscore = (probs * (dprob - delta) * scale).astype(BF16)
            grad_keys = dot_general(dscore, query, 1, 0)
            grads[0, h, here, :] = dot_general(keys, dscore, 0, 0).T.astype(BF16)
            if first:
                sums[0, h] = grad_keys
                sums[1, h] = grad_values
            elif final:
                grads[1, h] = (near[0, h] + (sums[0, h] + grad_keys)).astype(BF16)
                grads[2, h] = (near[1, h] + (sums[1, h] + grad_values)).astype(BF16)
            else:
                sums[0, h] += grad_keys
                sums[1, h] += grad_values

    own_rows = block(z, count)

    def heads_of(ref, at):
        return jnp.concatenate([ref[h, at, :] for h in range(4)], axis=1)

    def attended_term(f):
        return dot_general(heads_of(att, own_rows), wo_ref[:, block(f, half)], 1, 0)

    def token_term(f):
        total = None
        for j in range(3):
            term = dot_general(heads_of(grads.at[j], own_rows), w3_ref[j, block(f, half), :], 1, 1)
            total = term if total is None else total + term
        return total

    def term_copy(t, at, n):
        return remote(x_send.at[t, at], x_recv.at[t, at], st.at[n], rt.at[n], x_dev)

    t_copies = [
        term_copy(0, slice(0, count // 2), 0),
        term_copy(0, slice(count // 2, count), 1),
        term_copy(1, slice(0, count), 2),
    ]
    def share(u, at, n):
        return remote(own_w.at[u, at], other_w.at[u, at], sw.at[n], rw.at[n], c_dev)

    w_remote = [
        share(u, slice(r * half, (r + 1) * half), 2 * u + r) for u in range(3) for r in range(2)
    ] + [share(3, slice(0, 2 * half), 6)]
    width = w3_ref.shape[1]

    for p in range(PIECES):
        take_outer(T, MATE, p)
        take_inner(T, MATE, p)
    for p in range(PIECES):
        take_inner(T, NEXT, p)
        pl.when(jnp.logical_not(inner))(own_to_mate(G, p).start)
        pl.when(inner)(own_to_cross(G, p).start)
    wait_x(T, OWN)
    project(OWN)
    for p in range(PIECES):
        take_outer(T, NEXT, p)
        take_inner(T, LAST, p)
    for p in range(PIECES):
        pl.when(inner)(own_to_mate(G, p).start)
        pl.when(inner)(x_copy(G, OWN, p).start)
    wait_x(T, MATE)
    project(MATE)
    for p in range(PIECES):
        take_inner(G, MATE, p)
    for copy in label_copies:
        copy.wait_recv()
    for h in range(4):
        for b in range(4):
            row = marks[b, h : h + 1, :].astype(F32)
            label_rows[h, b] = row
            label_cols[h, b * count : (b + 1) * count, :] = jnp.broadcast_to(row, (HD, count)).T
    for p in range(PIECES):
        take_outer(T, LAST, p)
        take_inner(G, NEXT, p)
    for p in range(PIECES):
        pl.when(jnp.logical_not(inner))(x_copy(G, OWN, p).start)
    wait_x(T, NEXT)
    project(NEXT)
    for p in range(PIECES):
        take_inner(G, LAST, p)
    wait_x(T, LAST)
    project(LAST)
    forward(OWN)
    for p in range(PIECES // 2):
        take_outer(G, NEXT, p)
    forward(MATE)
    for p in range(PIECES // 2, PIECES):
        take_outer(G, NEXT, p)
    for p in range(PIECES):
        x_in(G, OWN, p).wait_recv()
        across(p).start()
    forward(NEXT)
    for p in range(PIECES // 2):
        take_outer(G, LAST, p)
    forward(LAST)
    for p in range(PIECES):
        take_outer(G, MATE, p)

    cotangents(OWN)
    backward(OWN, near, True)
    for p in range(PIECES // 2, PIECES):
        take_outer(G, LAST, p)
    x_send[0] = attended_term(other_x).astype(BF16)
    for copy in t_copies[:2]:
        copy.start()
    wait_x(G, NEXT)
    cotangents(NEXT)
    backward(NEXT, far, True)
    wait_x(G, MATE)
    cotangents(MATE)
    backward(MATE, near, False)
    x_own = [attended_term(x)]
    wait_x(G, LAST)
    cotangents(LAST)
    all_grads = grd[...].reshape(4 * count, width)
    value = dot_general(heads_of(att, slice(None)), all_grads, 0, 0)
    for f in range(2):
        own_w[3, f * half : (f + 1) * half, :] = value[:, f * half : (f + 1) * half].astype(BF16)
    w_remote[6].start()
    backward(LAST, far, False, True)
    x_send[1] = token_term(other_x).astype(BF16)
    t_copies[2].start()
    for j in range(3):
        grad = heads_of(grads.at[j], slice(None))
        for r in range(2):
            at = slice(r * half, (r + 1) * half)
            tokens = tok[:, :, at].reshape(4 * count, half)
            own_w[j, at, :] = dot_general(tokens, grad, 0, 0).astype(BF16)
            w_remote[2 * j + r].start()
    x_own.append(token_term(x))
    for copy in w_remote:
        copy.wait_recv()
    for t, target in ((0, att_out), (1, tokgrad_out)):
        for copy in (t_copies[:2], t_copies[2:])[t]:
            copy.wait_recv()
        target[...] = (x_own[t] + x_recv[t].astype(F32)).astype(BF16)

    for copy in [*label_copies, *w_remote, *t_copies]:
        copy.wait_send()
    for array in (T, G):
        for p in range(PIECES):
            own_to_mate(array, p).wait_send()
            for k in range(4):
                if (array, k) != (G, MATE):
                    x_copy(array, k, p).wait_send()
    for p in range(PIECES):
        across(p).wait_send()

    @pl.when(inner)
    def _():
        for array in (T, G):
            for p in range(PIECES):
                own_to_cross(array, p).wait_send()
                for k in (MATE, NEXT, LAST):
                    relay(array, k, p).wait_send()


def finish_sums(att_ref, tokgrad_ref, own_ref, other_ref, att_out, tokgrad_out, gwq_out, gwo_out, stage, sem):
    half = own_ref.shape[2]
    copies = [
        pltpu.make_async_copy(att_ref, att_out, sem.at[4]),
        pltpu.make_async_copy(tokgrad_ref, tokgrad_out, sem.at[5]),
    ]
    for u in range(4):
        if u < 3:
            stage[u] = own_ref[u].astype(F32) + other_ref[u].astype(F32)
            copies.append(pltpu.make_async_copy(stage.at[u], gwq_out.at[u], sem.at[u]))
        else:
            for f in range(2):
                at = slice(f * half, (f + 1) * half)
                stage[u, at, :] = own_ref[u, at, :].astype(F32) + other_ref[u, at, :].astype(F32)
                copies.append(pltpu.make_async_copy(stage.at[u, at], gwo_out.at[:, at], sem.at[(u, 6)[f]]))
                if f == 0:
                    copies[-1].start()
        if u == 0:
            copies[0].start()
            copies[1].start()
        copies[-1].start()
    for copy in copies:
        copy.wait()


def whole_layer(tokens, w_qkv, w_out, labels, grad_out):
    count, half = tokens.shape[1:]
    width = w_qkv.shape[0]
    size = w_out.shape[0]
    any_spec = pl.BlockSpec(memory_space=pl.ANY)
    dma = pltpu.SemaphoreType.DMA
    scratch = [
        pltpu.VMEM((3, width, size), BF16),
        pltpu.VMEM((size, width), BF16),
        pltpu.VMEM((4, count, width), BF16),
        pltpu.VMEM((4, count, width), BF16),
        pltpu.VMEM((3, 4, 4 * count, HD), BF16),
        pltpu.VMEM((4, 4, count, HD), BF16),
        pltpu.VMEM((4, 4, count), jnp.int32),
        pltpu.VMEM((4, 4, 1, count), F32),
        pltpu.VMEM((4, 4 * count, HD), F32),
        pltpu.VMEM((4, 4, 4 * count, count), F32),
        pltpu.VMEM((4, 4 * count, HD), BF16),
        pltpu.VMEM((2, 4, 4 * count, HD), F32),
        pltpu.VMEM((2, 4, 4 * count, HD), F32),
        pltpu.VMEM((3, 4, 4 * count, HD), BF16),
        pltpu.VMEM((2, count, half), BF16),
        pltpu.VMEM((2, count, half), BF16),
    ]
    for shape in ((2, 6, PIECES), (2, 4, PIECES), (2, 4, PIECES), (2, 4, PIECES), (3,), (3,), (7,), (7,), (3,), (3,), (4,)):
        scratch.append(dma(shape))
    partial = pl.pallas_call(
        layer_kernel,
        out_shape=[
            pltpu.VMEM((count, half), BF16),
            pltpu.VMEM((count, half), BF16),
            pltpu.VMEM((4, width, size), BF16),
            pltpu.VMEM((4, width, size), BF16),
        ],
        in_specs=[any_spec] * 4 + [VMEM_SPEC],
        out_specs=[VMEM_SPEC] * 4,
        scratch_shapes=scratch,
        compiler_params=pltpu.CompilerParams(
            collective_id=0, has_side_effects=True, vmem_limit_bytes=54 * 2**20
        ),
    )(tokens[0], grad_out[0], jnp.transpose(w_qkv, (1, 0, 2)), w_out, labels[0])
    attended, grad_tokens, grad_qkv, grad_w_out = pl.pallas_call(
        finish_sums,
        out_shape=[
            jax.ShapeDtypeStruct((count, half), BF16),
            jax.ShapeDtypeStruct((count, half), BF16),
            jax.ShapeDtypeStruct((3, width, size), F32),
            jax.ShapeDtypeStruct((size, width), F32),
        ],
        in_specs=[VMEM_SPEC] * 4,
        out_specs=[any_spec] * 4,
        scratch_shapes=[pltpu.VMEM((4, width, size), F32), dma((7,))],
        compiler_params=pltpu.CompilerParams(vmem_limit_bytes=24 * 2**20),
    )(*partial)
    return attended[None], grad_tokens[None], jnp.transpose(grad_qkv, (1, 0, 2)), grad_w_out


VMEM_SPEC = pl.BlockSpec(memory_space=pltpu.VMEM)


def call(kernel, shapes, scratch=(), **kw):
    return pl.pallas_call(
        kernel,
        out_shape=[jax.ShapeDtypeStruct(s, t) for s, t in shapes],
        out_specs=[VMEM_SPEC] * len(shapes),
        scratch_shapes=list(scratch),
        compiler_params=pltpu.CompilerParams(vmem_limit_bytes=56 * 2**20),
        **kw,
    )


def shards(tokens, w_qkv, w_out, labels, grad_out):
    heads = w_out.shape[0] // HD
    ctx_count = lax.axis_size("ctx")
    if (
        ctx_count == 4
        and heads == 4
        and lax.axis_size("tensor") == 2
        and lax.axis_size("dp") == 2
        and tokens.shape[1:] == (256, 512)
    ):
        return whole_layer(tokens, w_qkv, w_out, labels, grad_out)
    repeat = ctx_count // heads
    inner = [[g * heads + i for i in range(heads)] for g in range(repeat)]
    outer = [[g * heads + i for g in range(repeat)] for i in range(heads)]
    width = w_qkv.shape[0]
    size = heads * HD
    w_flat = w_qkv.reshape(width, 3 * size)

    marks_all = lax.all_gather(labels[0], "ctx", axis=1, tiled=True)
    rows = lax.all_gather(tokens, "tensor", axis=2, tiled=True)[0]
    grads = lax.all_gather(grad_out, "tensor", axis=2, tiled=True)[0]
    count = rows.shape[0]

    (packed,) = call(project_kernel, [((heads, count, 4 * HD), BF16)], in_specs=[VMEM_SPEC] * 4)(
        rows, grads, w_flat, w_out
    )
    me = lax.axis_index("ctx")
    head_of = me % heads
    exchange = functools.partial(
        lax.all_to_all, axis_name="ctx", split_axis=0, concat_axis=0, tiled=True, axis_index_groups=inner
    )
    mine = exchange(packed).reshape(heads * count, 4 * HD)
    total = heads * count
    key_marks = lax.dynamic_slice_in_dim(marks_all, head_of, 1, 0)
    row_marks = lax.dynamic_slice_in_dim(key_marks, (me // heads) * total, total, 1).reshape(total, 1)
    key_total = total * repeat
    block_rows = 256
    acc = [pltpu.VMEM((key_total, HD), F32)] * 2 if total // block_rows > 4 else [pltpu.VMEM((8, HD), F32)] * 2
    if repeat == 1:
        (back,) = call(
            functools.partial(attention_kernel, True, block_rows),
            [((total, 4 * HD), BF16)],
            acc,
            in_specs=[VMEM_SPEC] * 4,
        )(mine, mine[:8, : 2 * HD], row_marks, key_marks)
    else:
        keys_values = lax.all_gather(
            mine[:, HD : 3 * HD], "ctx", axis=0, tiled=True, axis_index_groups=outer
        )
        back, terms = call(
            functools.partial(attention_kernel, False, block_rows),
            [((total, 4 * HD), BF16), ((key_total, 2 * HD), BF16)],
            acc,
            in_specs=[VMEM_SPEC] * 4,
        )(mine, keys_values, row_marks, key_marks)
        summed = lax.psum_scatter(
            terms, "ctx", scatter_dimension=0, tiled=True, axis_index_groups=outer
        )
        back = jnp.concatenate([back[:, :HD], summed, back[:, 3 * HD :]], axis=1)
    home = exchange(back.reshape(heads, count, 4 * HD))
    out_terms, in_terms, grad_w_qkv, grad_w_out = call(
        finish_kernel,
        [
            ((count, width), BF16),
            ((count, width), BF16),
            ((width, 3 * size), BF16),
            ((size, width), BF16),
        ],
        in_specs=[VMEM_SPEC] * 5,
    )(home, rows, grads, w_flat, w_out)
    summed_qkv = lax.psum(grad_w_qkv, ("ctx", "dp")).astype(F32).reshape(width, 3, size)
    summed_out = lax.psum(grad_w_out, ("ctx", "dp")).astype(F32)
    attended = lax.psum_scatter(out_terms, "tensor", scatter_dimension=1, tiled=True)
    grad_tokens = lax.psum_scatter(in_terms, "tensor", scatter_dimension=1, tiled=True)
    return (attended[None], grad_tokens[None], summed_qkv, summed_out)


def solution(mesh):
    placed = (
        P(("groups", "dp"), "ctx", "tensor"),
        P(None, None, "tensor"),
        P("tensor", None),
        P(("groups", "dp"), "tensor", "ctx"),
        P(("groups", "dp"), "ctx", "tensor"),
    )
    return jax.shard_map(
        shards,
        mesh=mesh,
        in_specs=placed,
        out_specs=(
            P(("groups", "dp"), "ctx", "tensor"),
            P(("groups", "dp"), "ctx", "tensor"),
            P("groups", None, "tensor"),
            P(("groups", "tensor"), None),
        ),
        check_vma=False,
    )
```

```python
import functools

import jax
import jax.numpy as jnp
from jax import lax
from jax.experimental import pallas as pl
from jax.experimental.pallas import tpu as pltpu
from jax.sharding import PartitionSpec as P

HD = 128
F32 = jnp.float32
BF16 = jnp.bfloat16


def dot_general(left, right, left_dim, right_dim):
    return lax.dot_general(
        left, right, (((left_dim,), (right_dim,)), ((), ())), preferred_element_type=F32
    )


def project_kernel(rows_ref, grads_ref, w_qkv_ref, w_out_ref, out_ref):
    heads = out_ref.shape[0]
    size = heads * HD
    for j in range(3):
        part = dot_general(rows_ref[...], w_qkv_ref[:, j * size : (j + 1) * size], 1, 0).astype(BF16)
        for h in range(heads):
            out_ref[h, :, j * HD : (j + 1) * HD] = part[:, h * HD : (h + 1) * HD]
    part = dot_general(grads_ref[...], w_out_ref[...], 1, 1).astype(BF16)
    for h in range(heads):
        out_ref[h, :, 3 * HD :] = part[:, h * HD : (h + 1) * HD]


def attention_kernel(own_keys, block_rows, x_ref, kv_ref, mark_ref, key_mark_ref, *outs):
    if own_keys:
        (y_ref, gk_acc, gv_acc) = outs
        keys = x_ref[:, HD : 2 * HD]
        values = x_ref[:, 2 * HD : 3 * HD]
    else:
        (y_ref, gkv_ref, gk_acc, gv_acc) = outs
        keys = kv_ref[:, :HD]
        values = kv_ref[:, HD:]
    key_marks = key_mark_ref[...]
    count = x_ref.shape[0] // block_rows

    def one_block(b):
        rows = pl.ds(pl.multiple_of(b * block_rows, block_rows), block_rows)
        query = x_ref[rows, :HD]
        cot = x_ref[rows, 3 * HD :]
        scores = dot_general(query, keys, 1, 1) * HD ** (-0.5)
        scores = jnp.where(mark_ref[rows, :] == key_marks, scores, F32(-1e30))
        top = jnp.max(scores, axis=1, keepdims=True)
        expo = jnp.exp(scores - top)
        full = expo * (1.0 / jnp.sum(expo, axis=1, keepdims=True))
        probs = full.astype(BF16)
        attention = dot_general(probs, values, 1, 0).astype(BF16)
        dprob = dot_general(cot, values, 1, 1)
        delta = jnp.sum(cot.astype(F32) * attention.astype(F32), axis=1, keepdims=True)
        dscore = (full * (dprob - delta) * HD ** (-0.5)).astype(BF16)
        y_ref[rows, :HD] = dot_general(dscore, keys, 1, 0).astype(BF16)
        y_ref[rows, 3 * HD :] = attention
        return dot_general(dscore, query, 0, 0), dot_general(probs, cot, 0, 0)

    if count <= 4:
        grad_keys, grad_values = one_block(0)
        for b in range(1, count):
            more_keys, more_values = one_block(b)
            grad_keys = grad_keys + more_keys
            grad_values = grad_values + more_values
    else:
        gk_acc[...] = jnp.zeros_like(gk_acc)
        gv_acc[...] = jnp.zeros_like(gv_acc)

        @pl.loop(0, count)
        def _(b):
            more_keys, more_values = one_block(b)
            gk_acc[...] += more_keys
            gv_acc[...] += more_values

        grad_keys, grad_values = gk_acc[...], gv_acc[...]
    if own_keys:
        y_ref[:, HD : 2 * HD] = grad_keys.astype(BF16)
        y_ref[:, 2 * HD : 3 * HD] = grad_values.astype(BF16)
    else:
        gkv_ref[:, :HD] = grad_keys.astype(BF16)
        gkv_ref[:, HD:] = grad_values.astype(BF16)


def finish_kernel(z_ref, rows_ref, grads_ref, w_qkv_ref, w_out_ref, out_ref, in_ref, gwq_ref, gwo_ref):
    heads = z_ref.shape[0]
    size = heads * HD
    attention = jnp.concatenate([z_ref[h, :, 3 * HD :] for h in range(heads)], axis=1)
    out_ref[...] = dot_general(attention, w_out_ref[...], 1, 0).astype(BF16)
    gwo_ref[...] = dot_general(attention, grads_ref[...], 0, 0).astype(BF16)
    total = None
    for j in range(3):
        grad = jnp.concatenate([z_ref[h, :, j * HD : (j + 1) * HD] for h in range(heads)], axis=1)
        cols = slice(j * size, (j + 1) * size)
        term = dot_general(grad, w_qkv_ref[:, cols], 1, 1)
        total = term if total is None else total + term
        gwq_ref[:, cols] = dot_general(rows_ref[...], grad, 0, 0).astype(BF16)
    in_ref[...] = total.astype(BF16)


def remote(source, target, send_sem, recv_sem, device):
    return pltpu.make_async_remote_copy(
        src_ref=source,
        dst_ref=target,
        send_sem=send_sem,
        recv_sem=recv_sem,
        device_id=device,
        device_id_type=pl.DeviceIdType.MESH,
    )


LOG2E = 1.4426950408889634
PIECES = 2


def layer_kernel(
    tok_ref, gro_ref, w3_hbm, wo_hbm, lab_ref,
    att_out, tokgrad_out, own_w, other_w,
    w3_ref, wo_ref, tok, grd, qkv, cot, marks, label_rows, label_cols, probs_full, att,
    near, far, grads, x_send, x_recv,
    sz, rz, sx, rx, sl, rl, sw, rw, st, rt, wsem,
):
    z = lax.axis_index("ctx")
    x = lax.axis_index("tensor")
    c = lax.axis_index("dp")
    count, half = tok_ref.shape
    scale = HD ** (-0.5)
    other_x = 1 - x
    x_dev = {"tensor": other_x}
    c_dev = {"dp": 1 - c}
    peers = [lax.rem(z + d, 4) for d in range(1, 4)]
    side = z // 2
    mate = z + 1 - 2 * (z % 2)
    inner = jnp.logical_or(z == 1, z == 2)
    cross_dev = {"ctx": 3 - z}
    mate_dev = {"ctx": mate}
    places = (z, mate, 2 - side, 3 - 3 * side)
    OWN, MATE, NEXT, LAST = range(4)

    barrier = pltpu.get_barrier_semaphore()
    for device in [{"ctx": p} for p in peers] + [x_dev, c_dev]:
        pl.semaphore_signal(barrier, inc=1, device_id=device, device_id_type=pl.DeviceIdType.MESH)

    def block(index, size):
        return pl.ds(pl.multiple_of(index * size, size), size)

    local_copies = [
        pltpu.make_async_copy(w3_hbm, w3_ref, wsem.at[0]),
        pltpu.make_async_copy(wo_hbm, wo_ref, wsem.at[1]),
        pltpu.make_async_copy(tok_ref, tok.at[z, :, block(x, half)], wsem.at[2]),
        pltpu.make_async_copy(gro_ref, grd.at[z, :, block(x, half)], wsem.at[3]),
    ]
    for copy in local_copies:
        copy.start()
    pl.semaphore_wait(barrier, 5)

    piece = count // PIECES
    inputs = (tok_ref, gro_ref)
    gathered = (tok, grd)
    T, G = 0, 1
    mine = block(x, half)

    def rows(p):
        return slice(p * piece, (p + 1) * piece)

    def home(array, k, p):
        return gathered[array].at[places[k], rows(p), mine]

    def z_copy(array, k, p, slot, route, device):
        source = inputs[array].at[rows(p)] if k == OWN else home(array, k, p)
        return remote(source, home(array, k, p), sz.at[array, route, p], rz.at[array, slot, p], device)

    def z_in(array, k, p):
        return remote(home(array, k, p), home(array, k, p), sz.at[array, 0, p], rz.at[array, k, p], mate_dev)

    def x_copy(array, k, p):
        source = inputs[array].at[rows(p)] if k == OWN else home(array, k, p)
        return remote(source, home(array, k, p), sx.at[array, k, p], rx.at[array, k, p], x_dev)

    def x_in(array, k, p):
        there = gathered[array].at[places[k], rows(p), block(other_x, half)]
        return remote(there, there, sx.at[array, k, p], rx.at[array, k, p], x_dev)

    def own_to_mate(array, p):
        return z_copy(array, OWN, p, MATE, 0, mate_dev)

    def own_to_cross(array, p):
        return z_copy(array, OWN, p, NEXT, 1, cross_dev)

    def relay(array, k, p):
        if k == MATE:
            return z_copy(array, MATE, p, LAST, 2, cross_dev)
        return z_copy(array, k, p, k, k + 1, mate_dev)

    def across(p):
        there = grd.at[z, rows(p), block(other_x, half)]
        return remote(there, there, sz.at[G, 5, p], rz.at[G, OWN, p], mate_dev)

    def across_in(p):
        there = grd.at[mate, rows(p), block(other_x, half)]
        return remote(there, there, sz.at[G, 5, p], rz.at[G, OWN, p], mate_dev)

    def take_inner(array, k, p):
        @pl.when(inner)
        def _():
            z_in(array, k, p).wait_recv()
            relay(array, k, p).start()
            if (array, k) != (G, MATE):
                x_copy(array, k, p).start()

    def take_outer(array, k, p):
        @pl.when(jnp.logical_not(inner))
        def _():
            z_in(array, k, p).wait_recv()
            if (array, k) != (G, MATE):
                x_copy(array, k, p).start()

    def wait_x(array, k):
        for p in range(PIECES):
            if (array, k) == (G, MATE):
                across_in(p).wait_recv()
            else:
                x_in(array, k, p).wait_recv()

    for p in range(PIECES):
        own_to_mate(T, p).start()
        x_copy(T, OWN, p).start()

    @pl.when(inner)
    def _():
        for p in range(PIECES):
            own_to_cross(T, p).start()

    label_copies = []
    for d in range(3):
        label_copies.append(remote(lab_ref, marks.at[z], sl.at[d], rl.at[d], {"ctx": peers[d]}))
        label_copies[-1].start()
    marks[z] = lab_ref[...]
    for copy in local_copies:
        copy.wait()

    def project(k):
        here = block(places[k], count)
        tokens = tok[places[k]]
        for j in range(3):
            value = dot_general(tokens, w3_ref[j], 1, 0).astype(BF16)
            for h in range(4):
                qkv[j, h, here, :] = value[:, h * HD : (h + 1) * HD]

    def cotangents(k):
        value = dot_general(grd[places[k]], wo_ref[...], 1, 1).astype(BF16)
        for h in range(4):
            cot[h, places[k]] = value[:, h * HD : (h + 1) * HD]

    def mask(h, k):
        columns = label_cols[h]
        return jnp.concatenate([columns] * (count // HD), axis=1) == label_rows[h, places[k]]

    def reduce_rows(array, op):
        parts = array.reshape(8, array.shape[0] // 8, array.shape[1])
        return op(op(parts, axis=0), axis=0, keepdims=True)

    def forward(k):
        here = block(places[k], count)
        for h in range(4):
            scores = dot_general(qkv[1, h], qkv[0, h, here, :], 1, 1) * (scale * LOG2E)
            scores = jnp.where(mask(h, k), scores, F32(-1e30))
            expo = jnp.exp2(scores - reduce_rows(scores, jnp.max))
            probs = expo * (1.0 / reduce_rows(expo, jnp.sum))
            probs_full[h, k] = probs
            att[h, here, :] = dot_general(probs.astype(BF16), qkv[2, h], 0, 0).astype(BF16)

    def backward(k, sums, first, final=False):
        here = block(places[k], count)
        for h in range(4):
            keys, values, query = qkv[1, h], qkv[2, h], qkv[0, h, here, :]
            cotangent = cot[h, places[k]]
            product = cotangent.astype(F32) * att[h, here, :].astype(F32)
            delta = jnp.sum(product.T, axis=0, keepdims=True)
            probs = probs_full[h, k]
            grad_values = dot_general(probs.astype(BF16), cotangent, 1, 0)
            dprob = dot_general(values, cotangent, 1, 1)
            dscore = (probs * (dprob - delta) * scale).astype(BF16)
            grad_keys = dot_general(dscore, query, 1, 0)
            grads[0, h, here, :] = dot_general(keys, dscore, 0, 0).T.astype(BF16)
            if first:
                sums[0, h] = grad_keys
                sums[1, h] = grad_values
            elif final:
                grads[1, h] = (near[0, h] + (sums[0, h] + grad_keys)).astype(BF16)
                grads[2, h] = (near[1, h] + (sums[1, h] + grad_values)).astype(BF16)
            else:
                sums[0, h] += grad_keys
                sums[1, h] += grad_values

    own_rows = block(z, count)

    def heads_of(ref, at):
        return jnp.concatenate([ref[h, at, :] for h in range(4)], axis=1)

    def attended_term(f):
        return dot_general(heads_of(att, own_rows), wo_ref[:, block(f, half)], 1, 0)

    def token_term(f):
        total = None
        for j in range(3):
            term = dot_general(heads_of(grads.at[j], own_rows), w3_ref[j, block(f, half), :], 1, 1)
            total = term if total is None else total + term
        return total

    def term_copy(t, at, n):
        return remote(x_send.at[t, at], x_recv.at[t, at], st.at[n], rt.at[n], x_dev)

    t_copies = [
        term_copy(0, slice(0, count // 2), 0),
        term_copy(0, slice(count // 2, count), 1),
        term_copy(1, slice(0, count), 2),
    ]
    def share(u, at, n):
        return remote(own_w.at[u, at], other_w.at[u, at], sw.at[n], rw.at[n], c_dev)

    w_remote = [
        share(u, slice(r * half, (r + 1) * half), 2 * u + r) for u in range(3) for r in range(2)
    ] + [share(3, slice(0, 2 * half), 6)]
    width = w3_ref.shape[1]

    for p in range(PIECES):
        take_outer(T, MATE, p)
        take_inner(T, MATE, p)
    for p in range(PIECES):
        take_inner(T, NEXT, p)
        pl.when(jnp.logical_not(inner))(own_to_mate(G, p).start)
        pl.when(inner)(own_to_cross(G, p).start)
    wait_x(T, OWN)
    project(OWN)
    for p in range(PIECES):
        take_outer(T, NEXT, p)
        take_inner(T, LAST, p)
    for p in range(PIECES):
        pl.when(inner)(own_to_mate(G, p).start)
        pl.when(inner)(x_copy(G, OWN, p).start)
    wait_x(T, MATE)
    project(MATE)
    for p in range(PIECES):
        take_inner(G, MATE, p)
    for copy in label_copies:
        copy.wait_recv()
    for h in range(4):
        for b in range(4):
            row = marks[b, h : h + 1, :].astype(F32)
            label_rows[h, b] = row
            label_cols[h, b * count : (b + 1) * count, :] = jnp.broadcast_to(row, (HD, count)).T
    for p in range(PIECES):
        take_outer(T, LAST, p)
        take_inner(G, NEXT, p)
    for p in range(PIECES):
        pl.when(jnp.logical_not(inner))(x_copy(G, OWN, p).start)
    wait_x(T, NEXT)
    project(NEXT)
    for p in range(PIECES):
        take_inner(G, LAST, p)
    wait_x(T, LAST)
    project(LAST)
    forward(OWN)
    for p in range(PIECES // 2):
        take_outer(G, NEXT, p)
    forward(MATE)
    for p in range(PIECES // 2, PIECES):
        take_outer(G, NEXT, p)
    for p in range(PIECES):
        x_in(G, OWN, p).wait_recv()
        across(p).start()
    forward(NEXT)
    for p in range(PIECES // 2):
        take_outer(G, LAST, p)
    forward(LAST)
    for p in range(PIECES):
        take_outer(G, MATE, p)

    cotangents(OWN)
    backward(OWN, near, True)
    for p in range(PIECES // 2, PIECES):
        take_outer(G, LAST, p)
    x_send[0] = attended_term(other_x).astype(BF16)
    for copy in t_copies[:2]:
        copy.start()
    wait_x(G, NEXT)
    cotangents(NEXT)
    backward(NEXT, far, True)
    wait_x(G, MATE)
    cotangents(MATE)
    backward(MATE, near, False)
    x_own = [attended_term(x)]
    wait_x(G, LAST)
    cotangents(LAST)
    all_grads = grd[...].reshape(4 * count, width)
    value = dot_general(heads_of(att, slice(None)), all_grads, 0, 0)
    for f in range(2):
        own_w[3, f * half : (f + 1) * half, :] = value[:, f * half : (f + 1) * half].astype(BF16)
    w_remote[6].start()
    backward(LAST, far, False, True)
    for j in range(3):
        grad = heads_of(grads.at[j], slice(None))
        for r in range(2):
            at = slice(r * half, (r + 1) * half)
            tokens = tok[:, :, at].reshape(4 * count, half)
            own_w[j, at, :] = dot_general(tokens, grad, 0, 0).astype(BF16)
            w_remote[2 * j + r].start()
            if j == 0 and r == 0:
                x_send[1] = token_term(other_x).astype(BF16)
                t_copies[2].start()
    x_own.append(token_term(x))
    for t, target in ((0, att_out), (1, tokgrad_out)):
        for copy in (t_copies[:2], t_copies[2:])[t]:
            copy.wait_recv()
        target[...] = (x_own[t] + x_recv[t].astype(F32)).astype(BF16)

    for copy in w_remote:
        copy.wait_recv()
    for copy in [*label_copies, *w_remote, *t_copies]:
        copy.wait_send()
    for array in (T, G):
        for p in range(PIECES):
            own_to_mate(array, p).wait_send()
            for k in range(4):
                if (array, k) != (G, MATE):
                    x_copy(array, k, p).wait_send()
    for p in range(PIECES):
        across(p).wait_send()

    @pl.when(inner)
    def _():
        for array in (T, G):
            for p in range(PIECES):
                own_to_cross(array, p).wait_send()
                for k in (MATE, NEXT, LAST):
                    relay(array, k, p).wait_send()


def finish_sums(att_ref, tokgrad_ref, own_ref, other_ref, att_out, tokgrad_out, gwq_out, gwo_out, stage, sem):
    half = own_ref.shape[2]
    copies = [
        pltpu.make_async_copy(att_ref, att_out, sem.at[8]),
        pltpu.make_async_copy(tokgrad_ref, tokgrad_out, sem.at[9]),
    ]
    for copy in copies:
        copy.start()
    for u in range(4):
        for f in range(2):
            at = slice(f * half, (f + 1) * half)
            stage[u, at, :] = own_ref[u, at, :].astype(F32) + other_ref[u, at, :].astype(F32)
            target = gwq_out.at[u, at] if u < 3 else gwo_out.at[:, at]
            copies.append(pltpu.make_async_copy(stage.at[u, at], target, sem.at[2 * u + f]))
            copies[-1].start()
    for copy in copies:
        copy.wait()


def whole_layer(tokens, w_qkv, w_out, labels, grad_out):
    count, half = tokens.shape[1:]
    width = w_qkv.shape[0]
    size = w_out.shape[0]
    any_spec = pl.BlockSpec(memory_space=pl.ANY)
    dma = pltpu.SemaphoreType.DMA
    scratch = [
        pltpu.VMEM((3, width, size), BF16),
        pltpu.VMEM((size, width), BF16),
        pltpu.VMEM((4, count, width), BF16),
        pltpu.VMEM((4, count, width), BF16),
        pltpu.VMEM((3, 4, 4 * count, HD), BF16),
        pltpu.VMEM((4, 4, count, HD), BF16),
        pltpu.VMEM((4, 4, count), jnp.int32),
        pltpu.VMEM((4, 4, 1, count), F32),
        pltpu.VMEM((4, 4 * count, HD), F32),
        pltpu.VMEM((4, 4, 4 * count, count), F32),
        pltpu.VMEM((4, 4 * count, HD), BF16),
        pltpu.VMEM((2, 4, 4 * count, HD), F32),
        pltpu.VMEM((2, 4, 4 * count, HD), F32),
        pltpu.VMEM((3, 4, 4 * count, HD), BF16),
        pltpu.VMEM((2, count, half), BF16),
        pltpu.VMEM((2, count, half), BF16),
    ]
    for shape in ((2, 6, PIECES), (2, 4, PIECES), (2, 4, PIECES), (2, 4, PIECES), (3,), (3,), (7,), (7,), (3,), (3,), (4,)):
        scratch.append(dma(shape))
    partial = pl.pallas_call(
        layer_kernel,
        out_shape=[
            pltpu.VMEM((count, half), BF16),
            pltpu.VMEM((count, half), BF16),
            pltpu.VMEM((4, width, size), BF16),
            pltpu.VMEM((4, width, size), BF16),
        ],
        in_specs=[any_spec] * 4 + [VMEM_SPEC],
        out_specs=[VMEM_SPEC] * 4,
        scratch_shapes=scratch,
        compiler_params=pltpu.CompilerParams(
            collective_id=0, has_side_effects=True, vmem_limit_bytes=54 * 2**20
        ),
    )(tokens[0], grad_out[0], jnp.transpose(w_qkv, (1, 0, 2)), w_out, labels[0])
    attended, grad_tokens, grad_qkv, grad_w_out = pl.pallas_call(
        finish_sums,
        out_shape=[
            jax.ShapeDtypeStruct((count, half), BF16),
            jax.ShapeDtypeStruct((count, half), BF16),
            jax.ShapeDtypeStruct((3, width, size), F32),
            jax.ShapeDtypeStruct((size, width), F32),
        ],
        in_specs=[VMEM_SPEC] * 4,
        out_specs=[any_spec] * 4,
        scratch_shapes=[pltpu.VMEM((4, width, size), F32), dma((10,))],
        compiler_params=pltpu.CompilerParams(vmem_limit_bytes=24 * 2**20),
    )(*partial)
    return attended[None], grad_tokens[None], jnp.transpose(grad_qkv, (1, 0, 2)), grad_w_out


VMEM_SPEC = pl.BlockSpec(memory_space=pltpu.VMEM)


def call(kernel, shapes, scratch=(), **kw):
    return pl.pallas_call(
        kernel,
        out_shape=[jax.ShapeDtypeStruct(s, t) for s, t in shapes],
        out_specs=[VMEM_SPEC] * len(shapes),
        scratch_shapes=list(scratch),
        compiler_params=pltpu.CompilerParams(vmem_limit_bytes=56 * 2**20),
        **kw,
    )


def shards(tokens, w_qkv, w_out, labels, grad_out):
    heads = w_out.shape[0] // HD
    ctx_count = lax.axis_size("ctx")
    if (
        ctx_count == 4
        and heads == 4
        and lax.axis_size("tensor") == 2
        and lax.axis_size("dp") == 2
        and tokens.shape[1:] == (256, 512)
    ):
        return whole_layer(tokens, w_qkv, w_out, labels, grad_out)
    repeat = ctx_count // heads
    inner = [[g * heads + i for i in range(heads)] for g in range(repeat)]
    outer = [[g * heads + i for g in range(repeat)] for i in range(heads)]
    width = w_qkv.shape[0]
    size = heads * HD
    w_flat = w_qkv.reshape(width, 3 * size)

    marks_all = lax.all_gather(labels[0], "ctx", axis=1, tiled=True)
    rows = lax.all_gather(tokens, "tensor", axis=2, tiled=True)[0]
    grads = lax.all_gather(grad_out, "tensor", axis=2, tiled=True)[0]
    count = rows.shape[0]

    (packed,) = call(project_kernel, [((heads, count, 4 * HD), BF16)], in_specs=[VMEM_SPEC] * 4)(
        rows, grads, w_flat, w_out
    )
    me = lax.axis_index("ctx")
    head_of = me % heads
    exchange = functools.partial(
        lax.all_to_all, axis_name="ctx", split_axis=0, concat_axis=0, tiled=True, axis_index_groups=inner
    )
    mine = exchange(packed).reshape(heads * count, 4 * HD)
    total = heads * count
    key_marks = lax.dynamic_slice_in_dim(marks_all, head_of, 1, 0)
    row_marks = lax.dynamic_slice_in_dim(key_marks, (me // heads) * total, total, 1).reshape(total, 1)
    key_total = total * repeat
    block_rows = 256
    acc = [pltpu.VMEM((key_total, HD), F32)] * 2 if total // block_rows > 4 else [pltpu.VMEM((8, HD), F32)] * 2
    if repeat == 1:
        (back,) = call(
            functools.partial(attention_kernel, True, block_rows),
            [((total, 4 * HD), BF16)],
            acc,
            in_specs=[VMEM_SPEC] * 4,
        )(mine, mine[:8, : 2 * HD], row_marks, key_marks)
    else:
        keys_values = lax.all_gather(
            mine[:, HD : 3 * HD], "ctx", axis=0, tiled=True, axis_index_groups=outer
        )
        back, terms = call(
            functools.partial(attention_kernel, False, block_rows),
            [((total, 4 * HD), BF16), ((key_total, 2 * HD), BF16)],
            acc,
            in_specs=[VMEM_SPEC] * 4,
        )(mine, keys_values, row_marks, key_marks)
        summed = lax.psum_scatter(
            terms, "ctx", scatter_dimension=0, tiled=True, axis_index_groups=outer
        )
        back = jnp.concatenate([back[:, :HD], summed, back[:, 3 * HD :]], axis=1)
    home = exchange(back.reshape(heads, count, 4 * HD))
    out_terms, in_terms, grad_w_qkv, grad_w_out = call(
        finish_kernel,
        [
            ((count, width), BF16),
            ((count, width), BF16),
            ((width, 3 * size), BF16),
            ((size, width), BF16),
        ],
        in_specs=[VMEM_SPEC] * 5,
    )(home, rows, grads, w_flat, w_out)
    summed_qkv = lax.psum(grad_w_qkv, ("ctx", "dp")).astype(F32).reshape(width, 3, size)
    summed_out = lax.psum(grad_w_out, ("ctx", "dp")).astype(F32)
    attended = lax.psum_scatter(out_terms, "tensor", scatter_dimension=1, tiled=True)
    grad_tokens = lax.psum_scatter(in_terms, "tensor", scatter_dimension=1, tiled=True)
    return (attended[None], grad_tokens[None], summed_qkv, summed_out)


def solution(mesh):
    placed = (
        P(("groups", "dp"), "ctx", "tensor"),
        P(None, None, "tensor"),
        P("tensor", None),
        P(("groups", "dp"), "tensor", "ctx"),
        P(("groups", "dp"), "ctx", "tensor"),
    )
    return jax.shard_map(
        shards,
        mesh=mesh,
        in_specs=placed,
        out_specs=(
            P(("groups", "dp"), "ctx", "tensor"),
            P(("groups", "dp"), "ctx", "tensor"),
            P("groups", None, "tensor"),
            P(("groups", "tensor"), None),
        ),
        check_vma=False,
    )
```
